32 devices in a mesh: grp: 4 (over y, x), lm: 8 (over z, core).
Axes of the slice: x: 2, y: 2, z: 4, core: 2. Of those that a mesh axis runs over, the one named last changes fastest.
Arguments:
- embeddings: bfloat16 [8192, 512], P(('grp', 'lm')), may hold values from -14 to 14
- landmarks: bfloat16 [16384, 512], P('lm'), may hold values from -14 to 14
- start_vectors: float32 [8192, 128], P(('grp', 'lm')), may hold values from -10 to 10
- row_weight: float32 [8192], P(('grp', 'lm')), may hold values from 0.1 to 9
- spread: float32 [1], replicated, may hold values from 11.313708 to 33.941124
Outputs:
- subspace: float32 [8192, 128], P(('grp', 'lm'))
The draws below stay inside these ranges and needn't reach their ends.
All inputs are finite; a program needn't handle non-finite values.
Results may differ from the reference program's by a relative error of at most 0.019.
Values may be sent and summed in bfloat16 or wider, within the bound.
A program may use at most 128 MiB of HBM per device.

```python
import math
import jax
import jax.numpy as jnp
from jax import lax

D = 512
VECS = 128
ITERS = 2
ROWS = 8192
LANDMARKS = 16384


def draw_row_weight(key, part):
    position = jnp.arange(ROWS, dtype=jnp.float32) / ROWS
    base = jnp.exp(jax.random.uniform(key, (ROWS,), jnp.float32, math.log(0.1), 0.0))
    ramp = jnp.exp(position * math.log(3.0))
    return base * ramp


def feature_rows(key, count, salt):
    inner = jax.random.fold_in(key, salt)
    return jnp.clip(jax.random.normal(inner, (count, D), jnp.float32), -6.0, 6.0)


def draw_embeddings(key, part):
    return feature_rows(key, ROWS, 101).astype(jnp.bfloat16)


def draw_landmarks(key, part):
    return feature_rows(key, LANDMARKS, 202).astype(jnp.bfloat16)


def draw_start_vectors(key, part):
    first, second, third = jax.random.split(jax.random.fold_in(key, 17), 3)
    position = jnp.arange(ROWS, dtype=jnp.float32) / ROWS
    magnitude = jax.random.uniform(second, (1, VECS), jnp.float32, 1.0, 2.0)
    sign = 2.0 * jax.random.randint(third, (1, VECS), 0, 2).astype(jnp.float32) - 1.0
    column_factor = magnitude * sign
    noise = jnp.clip(jax.random.normal(first, (ROWS, VECS), jnp.float32), -6.0, 6.0)
    ramp = 0.5 * jnp.exp(position * math.log(3.0))
    return noise + ramp[:, None] * column_factor


def setup_inputs(seed: int = 0) -> dict:
    key_list = jax.random.split(jax.random.key(seed), 6)
    return {
        "embeddings": draw_embeddings(jax.random.fold_in(key_list[5], 71), 0),
        "landmarks": draw_landmarks(jax.random.fold_in(key_list[5], 71), 0),
        "start_vectors": draw_start_vectors(jax.random.fold_in(key_list[5], 71), 0),
        "row_weight": draw_row_weight(jax.random.fold_in(key_list[5], 71), 0),
        "spread": jnp.clip(jnp.exp(jax.random.uniform(key_list[4], (1,), jnp.float32, math.log(11.313708), math.log(33.941124))), 11.313708, 33.941124),
    }


def unit_rows(values):
    values = values.astype(jnp.float32)
    scale = lax.rsqrt(lax.optimization_barrier(jnp.sum(values * values, axis=1, keepdims=True)) + 1e-06)
    return (values * scale).astype(jnp.bfloat16)

def round_trip(values):
    rounded = lax.optimization_barrier(values.astype(jnp.bfloat16))
    return rounded.astype(jnp.float32)

def reference(embeddings, landmarks, start_vectors, row_weight, spread):
    highest = lax.Precision.HIGHEST
    rows_unit = unit_rows(embeddings).astype(jnp.float32)
    marks_unit = unit_rows(landmarks).astype(jnp.float32)
    total_rows = embeddings.shape[0]
    block = math.gcd(LANDMARKS, 1024)
    marks_blocks = marks_unit.reshape(LANDMARKS // block, block, D)
    gamma = spread[0]
    weight = row_weight.astype(jnp.float32)
    weight_sum = jnp.sum(weight)
    vectors = start_vectors.astype(jnp.float32)
    for step in range(ITERS):
        weighted_full = weight[:, None] * vectors
        weighted = round_trip(weighted_full)
        totals = lax.optimization_barrier(jnp.sum(weighted_full, axis=0))

        def visit(carry, marks):
            raw, shift = carry
            cosine = jnp.dot(rows_unit, marks.T, precision=highest)
            values = jnp.exp(gamma * cosine)
            kernel = round_trip(values)
            means = jnp.dot(weight, values, precision=highest) / weight_sum
            side = jnp.dot(kernel.T, weighted, precision=highest) - means[:, None] * totals[None, :]
            side_b = round_trip(side)
            raw = raw + jnp.dot(kernel, side_b, precision=highest)
            shift = shift + jnp.dot(means, side_b, precision=highest)
            return ((raw, shift), None)
        init = (jnp.zeros((total_rows, VECS), jnp.float32), jnp.zeros((VECS,), jnp.float32))
        (raw, shift), _ = lax.scan(visit, init, marks_blocks)
        image = weight[:, None] * (raw - shift[None, :])
        scale = jnp.sqrt(lax.optimization_barrier(jnp.mean(image * image, axis=0)) + 1e-06)
        vectors = image / scale[None, :]
    return vectors
```

```python
import functools

import jax
import jax.numpy as jnp
from jax import lax
from jax.experimental import pallas as pl
from jax.experimental.pallas import tpu as pltpu
from jax.sharding import PartitionSpec as P

ITERS = 2
HALVES = 2
F32 = jnp.float32
BF16 = jnp.bfloat16
BUILD = 1024
HIGHEST = lax.Precision.HIGHEST


def nt(a, b):
    return lax.dot_general(a, b, (((1,), (1,)), ((), ())), preferred_element_type=F32)


def nn(a, b):
    return jnp.dot(a, b, preferred_element_type=F32)


def tile(total, most):
    size = min(total, most)
    while total % size:
        size -= 8
    return size


def rows_at(index, size):
    return pl.ds(pl.multiple_of(index * size, size), size)


def column(row):
    return jnp.transpose(jnp.broadcast_to(row, (128, row.shape[1])))[:, 0:1]


def visits(z, line):
    left, right = z, line - 1 - z
    found = []
    for ahead, behind, from_left in ((left, right, True), (right, left, False)):
        for d in range(1, ahead + 1):
            if d == 1:
                key = 1 if ahead <= behind else 2
            elif d == 2:
                key = 0 if behind else 3
            else:
                key = d + 1
            found.append((key, d, from_left))
    return [(d, from_left) for _, d, from_left in sorted(found)]


def kernel(
    groups, members, spread_ref, emb_ref, marks_ref, vec_ref, weight_ref, out_ref,
    marks_in, marks_unit, kern_t, unit, wt, first_stats, stats, side, means, mean_rows,
    mean_all, side_out, side_in, side_acc, lead_out, lead_in, follow_out, follow_in,
    side_b, image_out, pair_in, line_out, line_in, held, norms, group_norms,
    row_sems, wt_sems, lead_sems, grp_sems, img_sems, norm_sems, mark_sems,
):
    own, width = emb_ref.shape
    marks = marks_ref.shape[0]
    vecs = vec_ref.shape[1]
    part = marks // groups
    line = members // 2
    total_rows = own * groups * members
    hv = vecs // HALVES
    me_g = lax.axis_index("grp")
    me_l = lax.axis_index("lm")
    z = me_l // 2
    c = me_l % 2
    sends = []
    half = own // 2

    def to(src, dst, send_sem, recv_sem, when=None, **device):
        copy = pltpu.make_async_remote_copy(
            src_ref=src, dst_ref=dst, send_sem=send_sem, recv_sem=recv_sem,
            device_id=device, device_id_type=pl.DeviceIdType.MESH,
        )
        if when is None:
            copy.start()
        else:
            pl.when(when)(copy.start)
        sends.append((when, copy))

    def arrived(ref, sem):
        pltpu.make_async_remote_copy(
            src_ref=ref, dst_ref=ref, send_sem=sem, recv_sem=sem,
            device_id={"lm": me_l}, device_id_type=pl.DeviceIdType.MESH,
        ).wait_recv()

    def mate():
        return z * 2 + 1 - c

    def along(k):
        return (z + k) % line * 2 + c

    def group(j):
        return (me_g + j) % groups

    order = sorted(range(1, line), key=lambda k: min(k, line - k))

    barrier = pltpu.get_barrier_semaphore()
    for k in range(1, members):
        pl.semaphore_signal(
            barrier, inc=1, device_id={"lm": (me_l + k) % members},
            device_id_type=pl.DeviceIdType.MESH,
        )
    for j in range(1, groups):
        pl.semaphore_signal(
            barrier, inc=1, device_id={"grp": group(j)}, device_id_type=pl.DeviceIdType.MESH
        )

    mark_copies = []
    for j in range(groups):
        mark_copies.append(pltpu.make_async_copy(
            marks_ref.at[pl.ds(pl.multiple_of(group(j) * part, part), part), :],
            marks_in.at[pl.ds(j * part, part), :], mark_sems.at[j],
        ))
        mark_copies[j].start()

    gamma = spread_ref[0]
    weight_row = weight_ref[...]
    values = emb_ref[...].astype(F32)
    scale = lax.rsqrt(jnp.sum(values * values, axis=1, keepdims=True) + 1e-06)
    unit[0] = (values * scale).astype(BF16)

    def stat_rows(columns):
        lane = lax.broadcasted_iota(jnp.int32, (columns[0].shape[0], 128), 1)
        wide = jnp.zeros(lane.shape, F32)
        for i, col in enumerate(columns):
            wide = jnp.where(lane == i, col, wide)
        return jnp.transpose(wide)[0:8, :]

    full = weight_row * jnp.transpose(vec_ref[...])
    first_stats[0] = jnp.zeros(first_stats.shape[1:], F32)
    first_stats[0, 0:1, 0:own] = weight_row
    for h in range(HALVES):
        piece = full[h * hv : (h + 1) * hv, :]
        wt[0, 0, h] = piece.astype(BF16)
        first_stats[0, 1 + h : 2 + h, 0:hv] = stat_rows(
            [jnp.sum(piece, axis=1, keepdims=True)]
        )[0:1, :]
    pl.semaphore_wait(barrier, members - 1 + groups - 1)

    def chunk(slot):
        return [
            (unit.at[slot, pl.ds(0, half), :], row_sems.at[0]),
            (unit.at[slot, pl.ds(half, half), :], row_sems.at[1]),
            (wt.at[0, slot], row_sems.at[2]),
            (first_stats.at[slot], row_sems.at[3]),
        ]

    for (src, sem), (dst, _) in zip(chunk(0), chunk(line)):
        to(src, dst, sem.at[2, 0], sem.at[0, line], lm=mate())
    for d in (2, 1):
        if d < line:
            for right in (1, 0):
                slot = line - d if right else d
                for (src, sem), (dst, _) in zip(chunk(0), chunk(slot)):
                    to(
                        src, dst, sem.at[1, line + 2 * (d - 1) + right], sem.at[0, slot],
                        when=z < line - d if right else z >= d,
                        lm=(z + d if right else z + line - d) % line * 2 + c,
                    )

    mark_tile = tile(part, 256)

    def unit_marks(i, carry):
        at = rows_at(i, mark_tile)
        block = marks_in[at, :].astype(F32)
        factor = lax.rsqrt(jnp.sum(block * block, axis=1, keepdims=True) + 1e-06)
        marks_unit[at, :] = (block * factor).astype(BF16)
        return carry

    for j in range(groups):
        mark_copies[j].wait()
        lax.fori_loop(
            j * part // mark_tile, (j + 1) * part // mark_tile, unit_marks, 0
        )

    def at_z(table):
        found = jnp.int32(table[0])
        for position in range(1, line):
            found = jnp.where(z == position, jnp.int32(table[position]), found)
        return found

    def relay(t):
        plan = [visits(position, line)[t] for position in range(line)]
        slot = at_z([line - d if left else d for d, left in plan])
        left = at_z([int(left) for _, left in plan]) == 1
        more = at_z([
            int(d >= 2 and (position < line - 1 if left else position > 0))
            for position, (d, left) in enumerate(plan)
        ]) == 1
        follow = jnp.where(more, jnp.where(left, slot - 1, slot + 1), slot)
        for (src, sem), (dst, _) in zip(chunk(slot), chunk(follow)):
            arrived(src, sem.at[0, slot])
            to(
                src, dst, sem.at[1, slot], sem.at[0, follow], when=more,
                lm=jnp.where(left, z + 1, z - 1 + line) % line * 2 + c,
            )
        for (src, sem), (dst, _) in zip(chunk(slot), chunk(line + slot)):
            to(src, dst, sem.at[2, slot], sem.at[0, line + slot], lm=mate())
        return slot

    def build(slot, first=False):
        here = pl.ds(pl.multiple_of(slot * own, own), own)

        def visit(i, carry):
            at = rows_at(i, build_tile)
            tall = jnp.exp(gamma * nt(marks_unit[at, :], unit[slot]))
            tall_b = tall.astype(BF16)
            kern_t[at, here] = tall_b
            scaled = tall * first_stats[slot, 0:1, 0:own]
            fold = scaled[:, 0:128]
            for piece in range(1, own // 128):
                fold = fold + scaled[:, piece * 128 : (piece + 1) * 128]
            product = nt(tall_b, wt[0, slot].reshape(vecs, own))
            if first:
                means[at, :] = fold
                side[at, :] = product
            else:
                means[at, :] += fold
                side[at, :] += product
            return carry

        lax.fori_loop(0, marks // build_tile, visit, 0)

    build_tile = tile(marks, BUILD)
    build(0, True)
    for ref, sem in chunk(line):
        arrived(ref, sem.at[0, line])
    build(line)
    for t in range(line - 1):
        slot = relay(t)
        build(slot)
        for ref, sem in chunk(line + slot):
            arrived(ref, sem.at[0, line + slot])
        build(line + slot)

    def parts():
        return [*range(1, groups), 0]

    def send_side(step, h, j):
        to(
            side_out.at[step, h, j], side_in.at[step, h, groups - j],
            grp_sems.at[step, h, 0, 1, j], grp_sems.at[step, h, 0, 0, groups - j],
            grp=group(j),
        )

    def first_side():
        weight_sum = jnp.zeros((1, 1), F32)
        rows = jnp.zeros((8, 128), F32)
        for slot in range(members):
            weight_sum = weight_sum + jnp.sum(
                first_stats[slot, 0:1, 0:own], axis=1, keepdims=True
            )
            rows = rows + first_stats[slot, :, 0:128]
        totals = [column(rows[1 + h : 2 + h, 0:128])[0:hv] for h in range(HALVES)]
        totals = jnp.concatenate(totals, axis=0)
        for j in parts():
            span = pl.ds(j * part, part)
            mean = jnp.sum(jnp.transpose(means[span, :]), axis=0, keepdims=True) / weight_sum
            mean_rows[j] = jnp.broadcast_to(mean, (8, part))
            block = jnp.transpose(side[span, :]) - totals * mean
            lead_out[j] = jnp.zeros(lead_out.shape[1:], F32)
            lead_out[j, 0:1, 0:part] = mean
            lead_out[j, 1:2, 0:128] = jnp.broadcast_to(weight_sum, (1, 128))
            lead_out[j, 2 : 2 + HALVES, 0:128] = rows[1 : 1 + HALVES, :]
            if j:
                to(
                    lead_out.at[j], lead_in.at[groups - j],
                    lead_sems.at[0, 1, j], lead_sems.at[0, 0, groups - j], grp=group(j),
                )
            for h in range(HALVES):
                piece = block[h * hv : (h + 1) * hv, :]
                if j:
                    side_out[0, h, j] = piece.astype(BF16)
                    if h == 0:
                        send_side(0, h, j)
                else:
                    side_acc[h, 0] = piece
        for h in range(1, HALVES):
            for j in range(1, groups):
                send_side(0, h, j)

    def line_chunk(step, h, slot):
        return [
            (wt.at[step, slot, h], wt_sems.at[step - 1, h, 0]),
            (stats.at[step - 1, h, slot], wt_sems.at[step - 1, h, 1]),
        ]

    def next_side(step, h):
        for k in order:
            back = line - k
            for (src, sem), (dst, _) in zip(
                line_chunk(step, h, back), line_chunk(step, h, line + back)
            ):
                arrived(src, sem.at[0, back])
                to(src, dst, sem.at[1, line + back], sem.at[0, line + back], lm=mate())

        def product(j, low):
            vectors = [wt[step, slot, h] for slot in range(low, low + line)]
            return nt(
                jnp.concatenate(vectors, axis=1),
                kern_t[j * part : (j + 1) * part, low * own : (low + line) * own],
            )

        for j in parts():
            side_acc[h, j] = product(j, 0)
        for slot in range(line, members):
            for ref, sem in line_chunk(step, h, slot):
                arrived(ref, sem.at[0, slot])
        rows = stats[step - 1, h, 0]
        for slot in range(1, members):
            rows = rows + stats[step - 1, h, slot]
        follow_out[step - 1, h] = rows
        for j in range(1, groups):
            to(
                follow_out.at[step - 1, h], follow_in.at[step - 1, h, groups - j],
                grp_sems.at[step, h, 2, 1, j], grp_sems.at[step, h, 2, 0, groups - j],
                grp=group(j),
            )
        totals = column(rows[0:1, :])[0:hv]
        for j in parts():
            block = side_acc[h, j] + product(j, line) - totals * mean_rows[j, 0:1, :]
            if j:
                side_out[step, h, j] = block.astype(BF16)
                send_side(step, h, j)
            else:
                side_acc[h, 0] = block

    def flat(rows, height):
        pad = -height % 8
        return jnp.concatenate(rows + [jnp.zeros_like(rows[0])] * pad, axis=0)

    def gather_side(step, h, shared):
        if step == 0 and h == 0:
            said = [lead_out[0]]
            for j in range(1, groups):
                arrived(lead_in.at[j], lead_sems.at[0, 0, j])
                said.append(lead_in[j])
            all_weight = sum(s[1:2, 0:1] for s in said)
            mean_row = sum(s[0:1, 0:part] * (s[1:2, 0:1] / all_weight) for s in said)
            mean_all[0] = jnp.broadcast_to(mean_row, (8, part))
            for j in range(1, groups):
                to(
                    mean_all.at[0], mean_all.at[groups - j],
                    lead_sems.at[1, 1, j], lead_sems.at[1, 0, groups - j], grp=group(j),
                )
            shared["gaps"] = flat([s[0:1, 0:part] - mean_row for s in said], groups)
            shared["totals"] = [
                [s[2 + i : 3 + i, 0:128] for s in said] for i in range(HALVES)
            ]
        factor = None
        if step == 0:
            totals = shared["totals"][h]
        else:
            said = [follow_out[step - 1, h]]
            for j in range(1, groups):
                arrived(follow_in.at[step - 1, h, j], grp_sems.at[step, h, 2, 0, j])
                said.append(follow_in[step - 1, h, j])
            totals = [s[0:1, :] for s in said]
            factor = column(
                1.0 / jnp.sqrt(sum(s[1:2, :] for s in said) / total_rows + 1e-06)
            )[0:hv]
        correction = lax.dot_general(
            flat(totals, groups), shared["gaps"],
            (((0,), (0,)), ((), ())), precision=HIGHEST, preferred_element_type=F32,
        )[0:hv]
        summed = side_acc[h, 0] + correction
        for j in range(1, groups):
            arrived(side_in.at[step, h, j], grp_sems.at[step, h, 0, 0, j])
            summed = summed + side_in[step, h, j].astype(F32)
        if factor is not None:
            summed = summed * factor
        side_b[step, h, 0] = summed.astype(BF16)
        for j in range(1, groups):
            to(
                side_b.at[step, h, 0], side_b.at[step, h, groups - j],
                grp_sems.at[step, h, 1, 1, j], grp_sems.at[step, h, 1, 0, groups - j],
                grp=group(j),
            )

    wide = 2 if line % 2 == 0 else 1

    def make_image(step, h):
        if step == 0 and h == 0:
            for j in range(1, groups):
                arrived(mean_all.at[j], lead_sems.at[1, 0, j])
        weighed = jnp.zeros((hv, part), F32)
        blocks = []
        for j in range(groups):
            if j:
                arrived(side_b.at[step, h, j], grp_sems.at[step, h, 1, 0, j])
            blocks.append(side_b[step, h, j])
            weighed = weighed + blocks[j].astype(F32) * mean_all[j, 0:1, :]
        shift = jnp.sum(weighed, axis=1, keepdims=True)
        whole = jnp.concatenate(blocks, axis=1)

        def product(slot):
            result = nn(whole, kern_t[:, slot * own : (slot + wide) * own]) - shift
            return [result[:, i * own : (i + 1) * own] for i in range(wide)]

        starts = range(line - wide, -1, -wide)
        for start in starts:
            pieces = product(line + start)
            for i in reversed(range(wide)):
                k = start + i
                image_out[step, h, k] = pieces[i].astype(BF16)
                to(
                    image_out.at[step, h, k], pair_in.at[step, h, k],
                    img_sems.at[step, h, 0, 1, k], img_sems.at[step, h, 0, 0, k], lm=mate(),
                )
        for start in starts:
            pieces = product(start)
            for i in reversed(range(wide)):
                k = start + i
                arrived(pair_in.at[step, h, k], img_sems.at[step, h, 0, 0, k])
                mine = pieces[i] + pair_in[step, h, k].astype(F32)
                if k == 0:
                    held[h] = mine
                    continue
                line_out[step, h, k] = mine.astype(BF16)
                to(
                    line_out.at[step, h, k], line_in.at[step, h, line - k],
                    img_sems.at[step, h, 1, 1, k], img_sems.at[step, h, 1, 0, line - k],
                    lm=along(k),
                )

    def end_image(step, h):
        image = held[h]
        for k in order:
            arrived(line_in.at[step, h, line - k], img_sems.at[step, h, 1, 0, line - k])
            image = image + line_in[step, h, line - k].astype(F32)
        image = weight_row * image
        square = jnp.sum(image * image, axis=1, keepdims=True)
        if step == ITERS - 1:
            held[h] = image
            return square
        full = weight_row * image
        wt[step + 1, 0, h] = full.astype(BF16)
        rows = stat_rows([jnp.sum(full, axis=1, keepdims=True), square])
        stats[step, h, 0] = jnp.zeros((8, 128), F32)
        stats[step, h, 0, :, 0:hv] = rows
        own_chunk = line_chunk(step + 1, h, 0)
        for (src, sem), (dst, _) in zip(own_chunk, line_chunk(step + 1, h, line)):
            to(src, dst, sem.at[1, 0], sem.at[0, line], lm=mate())
        for k in order:
            for (src, sem), (dst, _) in zip(own_chunk, line_chunk(step + 1, h, line - k)):
                to(src, dst, sem.at[1, k], sem.at[0, line - k], lm=along(k))
        return square

    shared = {}
    squares = []
    for step in range(ITERS):
        if step == 0:
            first_side()
        else:
            for h in range(HALVES):
                next_side(step, h)
        for h in range(HALVES):
            gather_side(step, h, shared)
        for h in range(HALVES):
            make_image(step, h)
        squares = [end_image(step, h) for h in range(HALVES)]

    square = stat_rows([jnp.concatenate(squares, axis=0)])[0:1, :]
    norms[0] = jnp.broadcast_to(square, norms.shape[1:])
    for k in range(1, members):
        back = members - k
        to(
            norms.at[0], norms.at[back], norm_sems.at[1, k], norm_sems.at[0, back],
            lm=(me_l + k) % members,
        )
    for k in range(1, members):
        arrived(norms.at[k], norm_sems.at[0, k])
        square = square + norms[k, 0:1, :]
    group_norms[0] = jnp.broadcast_to(square, norms.shape[1:])
    for j in range(1, groups):
        back = groups - j
        to(
            group_norms.at[0], group_norms.at[back],
            norm_sems.at[1, members + j], norm_sems.at[0, members + back], grp=group(j),
        )
    for j in range(1, groups):
        arrived(group_norms.at[j], norm_sems.at[0, members + j])
        square = square + group_norms[j, 0:1, :]
    image = jnp.transpose(jnp.concatenate([held[h] for h in range(HALVES)], axis=0))
    out_ref[...] = image / jnp.sqrt(square / total_rows + 1e-06)
    for when, copy in sends:
        if when is None:
            copy.wait_send()
        else:
            pl.when(when)(copy.wait_send)


def local(groups, members, embeddings, landmarks, start_vectors, row_weight, spread):
    own, width = embeddings.shape
    marks = landmarks.shape[0]
    vecs = start_vectors.shape[1]
    rows = own * members
    part = marks // groups
    line = members // 2
    hv = vecs // HALVES
    wide = max(own, 128)
    span = max(part, 128)
    vmem = pl.BlockSpec(memory_space=pltpu.VMEM)
    dma = pltpu.SemaphoreType.DMA
    return pl.pallas_call(
        functools.partial(kernel, groups, members),
        out_shape=jax.ShapeDtypeStruct((own, vecs), F32),
        in_specs=[pl.BlockSpec(memory_space=pltpu.SMEM), vmem, pl.BlockSpec(memory_space=pl.ANY), vmem, vmem],
        out_specs=vmem,
        scratch_shapes=[
            pltpu.VMEM((marks, width), BF16),
            pltpu.VMEM((marks, width), BF16),
            pltpu.VMEM((marks, rows), BF16),
            pltpu.VMEM((members, own, width), BF16),
            pltpu.VMEM((ITERS, members, HALVES, hv, own), BF16),
            pltpu.VMEM((members, 8, wide), F32),
            pltpu.VMEM((ITERS - 1, HALVES, members, 8, 128), F32),
            pltpu.VMEM((marks, vecs), F32),
            pltpu.VMEM((marks, 128), F32),
            pltpu.VMEM((groups, 8, part), F32),
            pltpu.VMEM((groups, 8, part), F32),
            pltpu.VMEM((ITERS, HALVES, groups, hv, part), BF16),
            pltpu.VMEM((ITERS, HALVES, groups, hv, part), BF16),
            pltpu.VMEM((HALVES, groups, hv, part), F32),
            pltpu.VMEM((groups, 8, span), F32),
            pltpu.VMEM((groups, 8, span), F32),
            pltpu.VMEM((ITERS - 1, HALVES, 8, 128), F32),
            pltpu.VMEM((ITERS - 1, HALVES, groups, 8, 128), F32),
            pltpu.VMEM((ITERS, HALVES, groups, hv, part), BF16),
            pltpu.VMEM((ITERS, HALVES, line, hv, own), BF16),
            pltpu.VMEM((ITERS, HALVES, line, hv, own), BF16),
            pltpu.VMEM((ITERS, HALVES, line, hv, own), BF16),
            pltpu.VMEM((ITERS, HALVES, line, hv, own), BF16),
            pltpu.VMEM((HALVES, hv, own), F32),
            pltpu.VMEM((members, 8, vecs), F32),
            pltpu.VMEM((groups, 8, vecs), F32),
            dma((4, 3, members + 4)),
            dma((ITERS - 1, HALVES, 2, 2, members)),
            dma((2, 2, groups)),
            dma((ITERS, HALVES, 3, 2, groups)),
            dma((ITERS, HALVES, 2, 2, line)),
            dma((2, members + groups)),
            dma((groups,)),
        ],
        compiler_params=pltpu.CompilerParams(
            collective_id=0, has_side_effects=True, vmem_limit_bytes=62 * 2**20
        ),
    )(spread, embeddings, landmarks, start_vectors, row_weight.reshape(1, own))


def solution(mesh):
    groups, members = mesh.shape["grp"], mesh.shape["lm"]
    in_specs = (
        P(("grp", "lm"), None),
        P("lm", None),
        P(("grp", "lm"), None),
        P(("grp", "lm")),
        P(),
    )
    return jax.shard_map(
        functools.partial(local, groups, members), mesh=mesh, in_specs=in_specs,
        out_specs=P(("grp", "lm"), None), check_vma=False,
    )
```

```python
import functools
import math

import jax
import jax.numpy as jnp
from jax import lax
from jax.experimental import pallas as pl
from jax.experimental.pallas import tpu as pltpu
from jax.sharding import PartitionSpec as P

ITERS = 2
HALVES = 2
F32 = jnp.float32
BF16 = jnp.bfloat16
BUILD = 1024
HIGHEST = lax.Precision.HIGHEST


def nt(a, b):
    return lax.dot_general(a, b, (((1,), (1,)), ((), ())), preferred_element_type=F32)


def nn(a, b):
    return jnp.dot(a, b, preferred_element_type=F32)


def tile(total, most):
    size = min(total, most)
    while total % size:
        size -= 8
    return size


def rows_at(index, size):
    return pl.ds(pl.multiple_of(index * size, size), size)


def column(row):
    return jnp.transpose(jnp.broadcast_to(row, (128, row.shape[1])))[:, 0:1]


def visits(z, line):
    left, right = z, line - 1 - z
    found = []
    for ahead, behind, from_left in ((left, right, True), (right, left, False)):
        for d in range(1, ahead + 1):
            if d == 1:
                key = 1 if ahead <= behind else 2
            elif d == 2:
                key = 0 if behind else 3
            else:
                key = d + 1
            found.append((key, d, from_left))
    return [(d, from_left) for _, d, from_left in sorted(found)]


def kernel(
    groups, members, spread_hbm, emb_hbm, marks_ref, vec_hbm, weight_hbm, out_ref,
    spread_ref, emb_ref, vec_ref, weight_ref, marks_in, marks_unit, kern_t, unit, wt, first_stats, stats, side, means, mean_rows,
    mean_all, side_out, side_in, side_acc, lead_out, lead_in, follow_out, follow_in,
    side_b, image_out, pair_in, line_out, line_in, held, norms, group_norms,
    row_sems, own_sems, wt_sems, lead_sems, grp_sems, img_sems, norm_sems, sent_sems,
    mark_sems, in_sems,
):
    own, width = emb_ref.shape
    marks = marks_ref.shape[0]
    vecs = vec_ref.shape[1]
    part = marks // groups
    line = members // 2
    total_rows = own * groups * members
    hv = vecs // HALVES
    me_g = lax.axis_index("grp")
    me_l = lax.axis_index("lm")
    z = me_l // 2
    c = me_l % 2
    half = own // 2
    sends = {}

    def size(ref):
        return math.prod(ref.shape) * jnp.dtype(ref.dtype).itemsize

    def to(src, dst, send_sem, recv_sem, when=None, **device):
        name, sem = send_sem
        copy = pltpu.make_async_remote_copy(
            src_ref=src, dst_ref=dst, send_sem=sem, recv_sem=recv_sem,
            device_id=device, device_id_type=pl.DeviceIdType.MESH,
        )
        if when is None:
            copy.start()
        else:
            pl.when(when)(copy.start)
        _, _, total = sends.get(name, (None, None, 0))
        sends[name] = (when, sem, total + size(src))

    def bytes_of(total):
        unit = 16 * 128 * 2
        blocks = total // unit
        across = 1
        while blocks % across or blocks // across > marks // 16:
            across += 1
        return kern_t.at[pl.ds(0, blocks // across * 16), pl.ds(0, across * 128)]

    def waiter(ref, sem):
        return pltpu.make_async_remote_copy(
            src_ref=ref, dst_ref=ref, send_sem=sem, recv_sem=sem,
            device_id={"lm": me_l}, device_id_type=pl.DeviceIdType.MESH,
        )

    def arrived(refs, sem):
        refs = refs if isinstance(refs, list) else [refs]
        ref = refs[0] if len(refs) == 1 else bytes_of(sum(map(size, refs)))
        waiter(ref, sem).wait_recv()

    def mate():
        return z * 2 + 1 - c

    def along(k):
        return (z + k) % line * 2 + c

    def group(j):
        return (me_g + j) % groups

    order = sorted(range(1, line), key=lambda k: min(k, line - k))

    barrier = pltpu.get_barrier_semaphore()
    for k in range(1, members):
        pl.semaphore_signal(
            barrier, inc=1, device_id={"lm": (me_l + k) % members},
            device_id_type=pl.DeviceIdType.MESH,
        )
    for j in range(1, groups):
        pl.semaphore_signal(
            barrier, inc=1, device_id={"grp": group(j)}, device_id_type=pl.DeviceIdType.MESH
        )

    inputs = []
    for i, (src, dst) in enumerate((
        (emb_hbm, emb_ref), (weight_hbm, weight_ref), (vec_hbm, vec_ref),
        (spread_hbm, spread_ref),
    )):
        inputs.append(pltpu.make_async_copy(src, dst, in_sems.at[i]))
        inputs[i].start()
    mark_copies = []
    for j in range(groups):
        mark_copies.append(pltpu.make_async_copy(
            marks_ref.at[pl.ds(pl.multiple_of(group(j) * part, part), part), :],
            marks_in.at[pl.ds(j * part, part), :], mark_sems.at[j],
        ))
        mark_copies[j].start()

    inputs[0].wait()
    values = emb_ref[...].astype(F32)
    scale = lax.rsqrt(jnp.sum(values * values, axis=1, keepdims=True) + 1e-06)
    unit[0] = (values * scale).astype(BF16)

    def stat_rows(columns):
        lane = lax.broadcasted_iota(jnp.int32, (columns[0].shape[0], 128), 1)
        wide = jnp.zeros(lane.shape, F32)
        for i, col in enumerate(columns):
            wide = jnp.where(lane == i, col, wide)
        return jnp.transpose(wide)[0:8, :]

    pl.semaphore_wait(barrier, members - 1 + groups - 1)

    def chunk(slot):
        return [
            ([unit.at[slot, pl.ds(0, half), :]], row_sems.at[0]),
            ([unit.at[slot, pl.ds(half, half), :]], row_sems.at[1]),
            ([wt.at[0, slot], first_stats.at[slot]], row_sems.at[2]),
        ]

    def send(sources, targets, name, sem, slot, when=None, **device):
        for (srcs, _), (dsts, recv) in zip(sources, targets):
            for src, dst in zip(srcs, dsts):
                to(src, dst, (name, sem), recv.at[slot], when, **device)

    def send_own(low, high):
        def pieces(slot):
            return chunk(slot)[low:high]

        send(pieces(0), pieces(line), "mate", own_sems.at[0], line, lm=mate())
        for d in (2, 1):
            if d < line:
                for right in (1, 0):
                    slot = line - d if right else d
                    send(
                        pieces(0), pieces(slot), f"own {d} {right}",
                        own_sems.at[2 * d + right - 1], slot,
                        when=z < line - d if right else z >= d,
                        lm=(z + d if right else z + line - d) % line * 2 + c,
                    )

    send_own(0, 2)
    for copy in inputs[1:]:
        copy.wait()
    gamma = spread_ref[0]
    weight_row = weight_ref[...]
    full = weight_row * jnp.transpose(vec_ref[...])
    first_stats[0] = jnp.zeros(first_stats.shape[1:], F32)
    first_stats[0, 0:1, 0:own] = weight_row
    for h in range(HALVES):
        piece = full[h * hv : (h + 1) * hv, :]
        wt[0, 0, h] = piece.astype(BF16)
        first_stats[0, 1 + h : 2 + h, 0:hv] = stat_rows(
            [jnp.sum(piece, axis=1, keepdims=True)]
        )[0:1, :]
    send_own(2, 3)

    mark_tile = tile(part, 256)

    def unit_marks(i, carry):
        at = rows_at(i, mark_tile)
        block = marks_in[at, :].astype(F32)
        factor = lax.rsqrt(jnp.sum(block * block, axis=1, keepdims=True) + 1e-06)
        marks_unit[at, :] = (block * factor).astype(BF16)
        return carry

    for j in range(groups):
        mark_copies[j].wait()
        lax.fori_loop(
            j * part // mark_tile, (j + 1) * part // mark_tile, unit_marks, 0
        )

    def at_z(table):
        found = jnp.int32(table[0])
        for position in range(1, line):
            found = jnp.where(z == position, jnp.int32(table[position]), found)
        return found

    def relay(t):
        plan = [visits(position, line)[t] for position in range(line)]
        slot = at_z([line - d if left else d for d, left in plan])
        left = at_z([int(left) for _, left in plan]) == 1
        more = at_z([
            int(d >= 2 and (position < line - 1 if left else position > 0))
            for position, (d, left) in enumerate(plan)
        ]) == 1
        follow = jnp.where(more, jnp.where(left, slot - 1, slot + 1), slot)
        for source, target in zip(chunk(slot), chunk(follow)):
            arrived(source[0], source[1].at[slot])
            send(
                [source], [target], f"relay {t}", own_sems.at[5 + t], follow, when=more,
                lm=jnp.where(left, z + 1, z - 1 + line) % line * 2 + c,
            )
        send(chunk(slot), chunk(line + slot), "mate", own_sems.at[0], line + slot, lm=mate())
        return slot

    def build(slot, first=False):
        here = pl.ds(pl.multiple_of(slot * own, own), own)

        def visit(i, carry):
            at = rows_at(i, build_tile)
            tall = jnp.exp(gamma * nt(marks_unit[at, :], unit[slot]))
            tall_b = tall.astype(BF16)
            kern_t[at, here] = tall_b
            scaled = tall * first_stats[slot, 0:1, 0:own]
            fold = scaled[:, 0:128]
            for piece in range(1, own // 128):
                fold = fold + scaled[:, piece * 128 : (piece + 1) * 128]
            product = nt(tall_b, wt[0, slot].reshape(vecs, own))
            if first:
                means[at, :] = fold
                side[at, :] = product
            else:
                means[at, :] += fold
                side[at, :] += product
            return carry

        lax.fori_loop(0, marks // build_tile, visit, 0)

    build_tile = tile(marks, BUILD)
    build(0, True)
    def await_mate(slot):
        for refs, sem in chunk(slot):
            arrived(refs, sem.at[slot])

    await_mate(line)
    build(line)
    for t in range(line - 1):
        slot = relay(t)
        build(slot)
        await_mate(line + slot)
        build(line + slot)

    def parts():
        return [*range(1, groups), 0]

    def send_side(step, h, j):
        to(
            side_out.at[step, h, j], side_in.at[step, h, groups - j],
            ("side", sent_sems.at[0]), grp_sems.at[h, 0, groups - j], grp=group(j),
        )

    def first_side():
        weight_sum = jnp.zeros((1, 1), F32)
        rows = jnp.zeros((8, 128), F32)
        for slot in range(members):
            weight_sum = weight_sum + jnp.sum(
                first_stats[slot, 0:1, 0:own], axis=1, keepdims=True
            )
            rows = rows + first_stats[slot, :, 0:128]
        totals = [column(rows[1 + h : 2 + h, 0:128])[0:hv] for h in range(HALVES)]
        totals = jnp.concatenate(totals, axis=0)
        for j in parts():
            span = pl.ds(j * part, part)
            mean = jnp.sum(jnp.transpose(means[span, :]), axis=0, keepdims=True) / weight_sum
            mean_rows[j] = jnp.broadcast_to(mean, (8, part))
            block = jnp.transpose(side[span, :]) - totals * mean
            lead_out[j] = jnp.zeros(lead_out.shape[1:], F32)
            lead_out[j, 0:1, 0:part] = mean
            lead_out[j, 1:2, 0:128] = jnp.broadcast_to(weight_sum, (1, 128))
            lead_out[j, 2 : 2 + HALVES, 0:128] = rows[1 : 1 + HALVES, :]
            if j:
                to(
                    lead_out.at[j], lead_in.at[groups - j],
                    ("lead", sent_sems.at[1]), lead_sems.at[0, groups - j], grp=group(j),
                )
            for h in range(HALVES):
                piece = block[h * hv : (h + 1) * hv, :]
                if j:
                    side_out[0, h, j] = piece.astype(BF16)
                    if h == 0:
                        send_side(0, h, j)
                else:
                    side_acc[h, 0] = piece
        for h in range(1, HALVES):
            for j in range(1, groups):
                send_side(0, h, j)

    def line_chunk(step, h, slot):
        return [wt.at[step, slot, h], stats.at[step - 1, h, slot]]

    def send_line(step, h, source, target, **device):
        for src, dst in zip(line_chunk(step, h, source), line_chunk(step, h, target)):
            to(src, dst, ("line", sent_sems.at[2]), wt_sems.at[h, target], **device)

    def next_side(step, h):
        for k in order:
            back = line - k
            arrived(line_chunk(step, h, back), wt_sems.at[h, back])
            send_line(step, h, back, line + back, lm=mate())

        def product(j, low):
            vectors = [wt[step, slot, h] for slot in range(low, low + line)]
            return nt(
                jnp.concatenate(vectors, axis=1),
                kern_t[j * part : (j + 1) * part, low * own : (low + line) * own],
            )

        for j in parts():
            side_acc[h, j] = product(j, 0)
        for slot in range(line, members):
            arrived(line_chunk(step, h, slot), wt_sems.at[h, slot])
        rows = stats[step - 1, h, 0]
        for slot in range(1, members):
            rows = rows + stats[step - 1, h, slot]
        follow_out[step - 1, h] = rows
        for j in range(1, groups):
            to(
                follow_out.at[step - 1, h], follow_in.at[step - 1, h, groups - j],
                ("follow", sent_sems.at[3]), grp_sems.at[h, 2, groups - j], grp=group(j),
            )
        totals = column(rows[0:1, :])[0:hv]
        for j in parts():
            block = side_acc[h, j] + product(j, line) - totals * mean_rows[j, 0:1, :]
            if j:
                side_out[step, h, j] = block.astype(BF16)
                send_side(step, h, j)
            else:
                side_acc[h, 0] = block

    def flat(rows, height):
        pad = -height % 8
        return jnp.concatenate(rows + [jnp.zeros_like(rows[0])] * pad, axis=0)

    def gather_side(step, h, shared):
        if step == 0 and h == 0:
            said = [lead_out[0]]
            for j in range(1, groups):
                arrived(lead_in.at[j], lead_sems.at[0, j])
                said.append(lead_in[j])
            all_weight = sum(s[1:2, 0:1] for s in said)
            mean_row = sum(s[0:1, 0:part] * (s[1:2, 0:1] / all_weight) for s in said)
            mean_all[0] = jnp.broadcast_to(mean_row, (8, part))
            for j in range(1, groups):
                to(
                    mean_all.at[0], mean_all.at[groups - j],
                    ("mean", sent_sems.at[4]), lead_sems.at[1, groups - j], grp=group(j),
                )
            shared["gaps"] = flat([s[0:1, 0:part] - mean_row for s in said], groups)
            shared["totals"] = [
                [s[2 + i : 3 + i, 0:128] for s in said] for i in range(HALVES)
            ]
        factor = None
        if step == 0:
            totals = shared["totals"][h]
        else:
            said = [follow_out[step - 1, h]]
            for j in range(1, groups):
                arrived(follow_in.at[step - 1, h, j], grp_sems.at[h, 2, j])
                said.append(follow_in[step - 1, h, j])
            totals = [s[0:1, :] for s in said]
            factor = column(
                1.0 / jnp.sqrt(sum(s[1:2, :] for s in said) / total_rows + 1e-06)
            )[0:hv]
        correction = lax.dot_general(
            flat(totals, groups), shared["gaps"],
            (((0,), (0,)), ((), ())), precision=HIGHEST, preferred_element_type=F32,
        )[0:hv]
        summed = side_acc[h, 0] + correction
        for j in range(1, groups):
            arrived(side_in.at[step, h, j], grp_sems.at[h, 0, j])
            summed = summed + side_in[step, h, j].astype(F32)
        if factor is not None:
            summed = summed * factor
        side_b[step, h, 0] = summed.astype(BF16)
        for j in range(1, groups):
            to(
                side_b.at[step, h, 0], side_b.at[step, h, groups - j],
                ("gather", sent_sems.at[5]), grp_sems.at[h, 1, groups - j], grp=group(j),
            )

    wide = 2 if line % 2 == 0 else 1

    def make_image(step, h):
        if step == 0 and h == 0:
            for j in range(1, groups):
                arrived(mean_all.at[j], lead_sems.at[1, j])
        weighed = jnp.zeros((hv, part), F32)
        blocks = []
        for j in range(groups):
            if j:
                arrived(side_b.at[step, h, j], grp_sems.at[h, 1, j])
            blocks.append(side_b[step, h, j])
            weighed = weighed + blocks[j].astype(F32) * mean_all[j, 0:1, :]
        shift = jnp.sum(weighed, axis=1, keepdims=True)
        whole = jnp.concatenate(blocks, axis=1)

        def product(slot):
            result = nn(whole, kern_t[:, slot * own : (slot + wide) * own]) - shift
            return [result[:, i * own : (i + 1) * own] for i in range(wide)]

        starts = range(line - wide, -1, -wide)
        for start in starts:
            pieces = product(line + start)
            for i in reversed(range(wide)):
                k = start + i
                image_out[step, h, k] = pieces[i].astype(BF16)
                to(
                    image_out.at[step, h, k], pair_in.at[step, h, k],
                    ("pair", sent_sems.at[6]), img_sems.at[h, 0, k], lm=mate(),
                )
        for start in starts:
            pieces = product(start)
            for i in reversed(range(wide)):
                k = start + i
                arrived(pair_in.at[step, h, k], img_sems.at[h, 0, k])
                mine = pieces[i] + pair_in[step, h, k].astype(F32)
                if k == 0:
                    held[h] = mine
                    continue
                line_out[step, h, k] = mine.astype(BF16)
                to(
                    line_out.at[step, h, k], line_in.at[step, h, line - k],
                    ("sum", sent_sems.at[7]), img_sems.at[h, 1, line - k], lm=along(k),
                )

    def end_image(step, h):
        image = held[h]
        for k in order:
            arrived(line_in.at[step, h, line - k], img_sems.at[h, 1, line - k])
            image = image + line_in[step, h, line - k].astype(F32)
        image = weight_row * image
        square = jnp.sum(image * image, axis=1, keepdims=True)
        if step == ITERS - 1:
            held[h] = image
            return square
        full = weight_row * image
        wt[step + 1, 0, h] = full.astype(BF16)
        rows = stat_rows([jnp.sum(full, axis=1, keepdims=True), square])
        stats[step, h, 0] = jnp.zeros((8, 128), F32)
        stats[step, h, 0, :, 0:hv] = rows
        send_line(step + 1, h, 0, line, lm=mate())
        for k in order:
            send_line(step + 1, h, 0, line - k, lm=along(k))
        return square

    shared = {}
    squares = []
    for step in range(ITERS):
        if step == 0:
            first_side()
        else:
            for h in range(HALVES):
                next_side(step, h)
        for h in range(HALVES):
            gather_side(step, h, shared)
        for h in range(HALVES):
            make_image(step, h)
        squares = [end_image(step, h) for h in range(HALVES)]

    square = stat_rows([jnp.concatenate(squares, axis=0)])[0:1, :]
    norms[0] = jnp.broadcast_to(square, norms.shape[1:])
    for k in range(1, members):
        back = members - k
        to(
            norms.at[0], norms.at[back], ("norm", sent_sems.at[8]), norm_sems.at[back],
            lm=(me_l + k) % members,
        )
    for k in range(1, members):
        arrived(norms.at[k], norm_sems.at[k])
        square = square + norms[k, 0:1, :]
    group_norms[0] = jnp.broadcast_to(square, norms.shape[1:])
    for j in range(1, groups):
        back = groups - j
        to(
            group_norms.at[0], group_norms.at[back],
            ("norm", sent_sems.at[8]), norm_sems.at[members + back], grp=group(j),
        )
    for j in range(1, groups):
        arrived(group_norms.at[j], norm_sems.at[members + j])
        square = square + group_norms[j, 0:1, :]
    image = jnp.transpose(jnp.concatenate([held[h] for h in range(HALVES)], axis=0))
    out_ref[...] = image / jnp.sqrt(square / total_rows + 1e-06)
    for when, sem, total in sends.values():
        wait = waiter(bytes_of(total), sem).wait_send
        if when is None:
            wait()
        else:
            pl.when(when)(wait)


def local(groups, members, embeddings, landmarks, start_vectors, row_weight, spread):
    own, width = embeddings.shape
    marks = landmarks.shape[0]
    vecs = start_vectors.shape[1]
    rows = own * members
    part = marks // groups
    line = members // 2
    hv = vecs // HALVES
    wide = max(own, 128)
    span = max(part, 128)
    vmem = pl.BlockSpec(memory_space=pltpu.VMEM)
    dma = pltpu.SemaphoreType.DMA
    return pl.pallas_call(
        functools.partial(kernel, groups, members),
        out_shape=jax.ShapeDtypeStruct((own, vecs), F32),
        in_specs=[pl.BlockSpec(memory_space=pl.ANY)] * 5,
        out_specs=vmem,
        scratch_shapes=[
            pltpu.SMEM((1,), F32),
            pltpu.VMEM((own, width), BF16),
            pltpu.VMEM((own, vecs), F32),
            pltpu.VMEM((1, own), F32),
            pltpu.VMEM((marks, width), BF16),
            pltpu.VMEM((marks, width), BF16),
            pltpu.VMEM((marks, rows), BF16),
            pltpu.VMEM((members, own, width), BF16),
            pltpu.VMEM((ITERS, members, HALVES, hv, own), BF16),
            pltpu.VMEM((members, 8, wide), F32),
            pltpu.VMEM((ITERS - 1, HALVES, members, 8, 128), F32),
            pltpu.VMEM((marks, vecs), F32),
            pltpu.VMEM((marks, 128), F32),
            pltpu.VMEM((groups, 8, part), F32),
            pltpu.VMEM((groups, 8, part), F32),
            pltpu.VMEM((ITERS, HALVES, groups, hv, part), BF16),
            pltpu.VMEM((ITERS, HALVES, groups, hv, part), BF16),
            pltpu.VMEM((HALVES, groups, hv, part), F32),
            pltpu.VMEM((groups, 8, span), F32),
            pltpu.VMEM((groups, 8, span), F32),
            pltpu.VMEM((ITERS - 1, HALVES, 8, 128), F32),
            pltpu.VMEM((ITERS - 1, HALVES, groups, 8, 128), F32),
            pltpu.VMEM((ITERS, HALVES, groups, hv, part), BF16),
            pltpu.VMEM((ITERS, HALVES, line, hv, own), BF16),
            pltpu.VMEM((ITERS, HALVES, line, hv, own), BF16),
            pltpu.VMEM((ITERS, HALVES, line, hv, own), BF16),
            pltpu.VMEM((ITERS, HALVES, line, hv, own), BF16),
            pltpu.VMEM((HALVES, hv, own), F32),
            pltpu.VMEM((members, 8, vecs), F32),
            pltpu.VMEM((groups, 8, vecs), F32),
            dma((3, members)),
            dma((5 + line,)),
            dma((HALVES, members)),
            dma((2, groups)),
            dma((HALVES, 3, groups)),
            dma((HALVES, 2, line)),
            dma((members + groups,)),
            dma((9,)),
            dma((groups,)),
            dma((4,)),
        ],
        compiler_params=pltpu.CompilerParams(
            collective_id=0, has_side_effects=True, vmem_limit_bytes=62 * 2**20
        ),
    )(spread, embeddings, landmarks, start_vectors, row_weight.reshape(1, own))


def solution(mesh):
    groups, members = mesh.shape["grp"], mesh.shape["lm"]
    in_specs = (
        P(("grp", "lm"), None),
        P("lm", None),
        P(("grp", "lm"), None),
        P(("grp", "lm")),
        P(),
    )
    return jax.shard_map(
        functools.partial(local, groups, members), mesh=mesh, in_specs=in_specs,
        out_specs=P(("grp", "lm"), None), check_vma=False,
    )
```

```python
import functools
import math

import jax
import jax.numpy as jnp
from jax import lax
from jax.experimental import pallas as pl
from jax.experimental.pallas import tpu as pltpu
from jax.sharding import PartitionSpec as P

ITERS = 2
HALVES = 2
SUBS = 2
F32 = jnp.float32
BF16 = jnp.bfloat16
BUILD = 1024
HIGHEST = lax.Precision.HIGHEST


def nt(a, b):
    return lax.dot_general(a, b, (((1,), (1,)), ((), ())), preferred_element_type=F32)


def nn(a, b):
    return jnp.dot(a, b, preferred_element_type=F32)


def tile(total, most):
    size = min(total, most)
    while total % size:
        size -= 8
    return size


def rows_at(index, size):
    return pl.ds(pl.multiple_of(index * size, size), size)


def column(row):
    return jnp.transpose(jnp.broadcast_to(row, (128, row.shape[1])))[:, 0:1]


def visits(z, line):
    left, right = z, line - 1 - z
    found = []
    for ahead, behind, from_left in ((left, right, True), (right, left, False)):
        for d in range(1, ahead + 1):
            if d == 1:
                key = 1 if ahead <= behind else 2
            elif d == 2:
                key = 0 if behind else line + 1
            else:
                key = d + 1
            found.append((key, d, from_left))
    return [(d, from_left) for _, d, from_left in sorted(found)]


def kernel(
    groups, members, spread_hbm, emb_hbm, marks_ref, vec_hbm, weight_hbm, out_ref,
    spread_ref, emb_ref, vec_ref, weight_ref, marks_in, marks_unit, kern_t, unit, wt, first_stats, stats, side, means, mean_rows,
    mean_all, side_out, side_in, side_acc, lead_out, lead_in, follow_out, follow_in,
    side_b, image_out, pair_in, line_out, line_in, held, norms, gauge,
    row_sems, own_sems, wt_sems, lead_sems, grp_sems, img_sems, norm_sems, sent_sems,
    mark_sems, in_sems,
):
    own, width = emb_ref.shape
    marks = marks_ref.shape[0]
    vecs = vec_ref.shape[1]
    part = marks // groups
    line = members // 2
    total_rows = own * groups * members
    hv = vecs // HALVES
    me_g = lax.axis_index("grp")
    me_l = lax.axis_index("lm")
    z = me_l // 2
    c = me_l % 2
    half = own // 2
    cut = part // SUBS
    sends = {}

    def size(ref):
        return math.prod(ref.shape) * jnp.dtype(ref.dtype).itemsize

    def to(src, dst, send_sem, recv_sem, when=None, **device):
        name, sem = send_sem
        copy = pltpu.make_async_remote_copy(
            src_ref=src, dst_ref=dst, send_sem=sem, recv_sem=recv_sem,
            device_id=device, device_id_type=pl.DeviceIdType.MESH,
        )
        if when is None:
            copy.start()
        else:
            pl.when(when)(copy.start)
        _, _, total = sends.get(name, (None, None, 0))
        sends[name] = (when, sem, total + size(src))

    def bytes_of(total):
        unit = 16 * 128 * 2
        if total % unit:
            return gauge.at[pl.ds(0, total // 512)]
        blocks = total // unit
        across = 1
        while blocks % across or blocks // across > marks // 16:
            across += 1
        return kern_t.at[pl.ds(0, blocks // across * 16), pl.ds(0, across * 128)]

    def waiter(ref, sem):
        return pltpu.make_async_remote_copy(
            src_ref=ref, dst_ref=ref, send_sem=sem, recv_sem=sem,
            device_id={"lm": me_l}, device_id_type=pl.DeviceIdType.MESH,
        )

    def arrived(refs, sem):
        refs = refs if isinstance(refs, list) else [refs]
        ref = refs[0] if len(refs) == 1 else bytes_of(sum(map(size, refs)))
        waiter(ref, sem).wait_recv()

    def mate():
        return z * 2 + 1 - c

    def along(k):
        return (z + k) % line * 2 + c

    def group(j):
        return (me_g + j) % groups

    order = sorted(range(1, line), key=lambda k: min(k, line - k))

    barrier = pltpu.get_barrier_semaphore()
    for k in range(1, members):
        pl.semaphore_signal(
            barrier, inc=1, device_id={"lm": (me_l + k) % members},
            device_id_type=pl.DeviceIdType.MESH,
        )
    for j in range(1, groups):
        pl.semaphore_signal(
            barrier, inc=1, device_id={"grp": group(j)}, device_id_type=pl.DeviceIdType.MESH
        )

    inputs = []
    for i, (src, dst) in enumerate((
        (emb_hbm, emb_ref), (weight_hbm, weight_ref), (vec_hbm, vec_ref),
        (spread_hbm, spread_ref),
    )):
        inputs.append(pltpu.make_async_copy(src, dst, in_sems.at[i]))
        inputs[i].start()
    mark_copies = []
    for j in range(groups):
        mark_copies.append(pltpu.make_async_copy(
            marks_ref.at[pl.ds(pl.multiple_of(group(j) * part, part), part), :],
            marks_in.at[pl.ds(j * part, part), :], mark_sems.at[j],
        ))
        mark_copies[j].start()

    inputs[0].wait()
    values = emb_ref[...].astype(F32)
    scale = lax.rsqrt(jnp.sum(values * values, axis=1, keepdims=True) + 1e-06)
    unit[0] = (values * scale).astype(BF16)

    def stat_rows(columns):
        lane = lax.broadcasted_iota(jnp.int32, (columns[0].shape[0], 128), 1)
        wide = jnp.zeros(lane.shape, F32)
        for i, col in enumerate(columns):
            wide = jnp.where(lane == i, col, wide)
        return jnp.transpose(wide)[0:8, :]

    for copy in inputs[1:]:
        copy.wait()
    gamma = spread_ref[0]
    weight_row = weight_ref[...]
    full = weight_row * jnp.transpose(vec_ref[...])
    first_stats[0] = jnp.zeros(first_stats.shape[1:], F32)
    first_stats[0, 0:1, 0:own] = weight_row
    for h in range(HALVES):
        piece = full[h * hv : (h + 1) * hv, :]
        wt[0, 0, h] = piece.astype(BF16)
        first_stats[0, 1 + h : 2 + h, 0:hv] = stat_rows(
            [jnp.sum(piece, axis=1, keepdims=True)]
        )[0:1, :]
    pl.semaphore_wait(barrier, members - 1 + groups - 1)

    def chunk(slot):
        return [
            ([wt.at[0, slot], first_stats.at[slot]], row_sems.at[0]),
            ([unit.at[slot, pl.ds(0, half), :]], row_sems.at[1]),
            ([unit.at[slot, pl.ds(half, half), :]], row_sems.at[2]),
        ]

    def send(sources, targets, name, sem, slot, when=None, **device):
        for (srcs, _), (dsts, recv) in zip(sources, targets):
            for src, dst in zip(srcs, dsts):
                to(src, dst, (name, sem), recv.at[slot], when, **device)

    def send_own():
        send(chunk(0), chunk(line), "mate", own_sems.at[0], line, lm=mate())
        for d, early in ((2, True), (1, False), (2, False)):
            if d < line:
                for right in (1, 0):
                    slot = line - d if right else d
                    goes = z < line - d if right else z >= d
                    relayed = z < line - 3 if right else z >= 3
                    if d == 2:
                        goes = relayed if early else goes & ~relayed
                    send(
                        chunk(0), chunk(slot), f"own {d} {right} {early}",
                        own_sems.at[2 * d + right - 1], slot, when=goes,
                        lm=(z + d if right else z + line - d) % line * 2 + c,
                    )

    send_own()

    mark_tile = tile(part, 256)

    def unit_marks(i, carry):
        at = rows_at(i, mark_tile)
        block = marks_in[at, :].astype(F32)
        factor = lax.rsqrt(jnp.sum(block * block, axis=1, keepdims=True) + 1e-06)
        marks_unit[at, :] = (block * factor).astype(BF16)
        return carry

    for j in range(groups):
        mark_copies[j].wait()
        lax.fori_loop(
            j * part // mark_tile, (j + 1) * part // mark_tile, unit_marks, 0
        )

    def at_z(table):
        found = jnp.int32(table[0])
        for position in range(1, line):
            found = jnp.where(z == position, jnp.int32(table[position]), found)
        return found

    def relay(t, low=0, high=3):
        plan = [visits(position, line)[t] for position in range(line)]
        slot = at_z([line - d if left else d for d, left in plan])
        left = at_z([int(left) for _, left in plan]) == 1
        more = at_z([
            int(d >= 2 and (position < line - 1 if left else position > 0))
            for position, (d, left) in enumerate(plan)
        ]) == 1
        follow = jnp.where(more, jnp.where(left, slot - 1, slot + 1), slot)
        for source, target in zip(chunk(slot)[low:high], chunk(follow)[low:high]):
            arrived(source[0], source[1].at[slot])
            send(
                [source], [target], f"relay {t}", own_sems.at[5 + t], follow, when=more,
                lm=jnp.where(left, z + 1, z - 1 + line) % line * 2 + c,
            )
        send(
            chunk(slot)[low:high], chunk(line + slot)[low:high], "mate", own_sems.at[0],
            line + slot, lm=mate(),
        )
        return slot

    def build(slot, low=0, high=own):
        count = high - low
        here = pl.ds(pl.multiple_of(slot * own + low, math.gcd(own, 128)), count)

        def visit(i, carry):
            at = rows_at(i, build_tile)
            tall = jnp.exp(gamma * nt(marks_unit[at, :], unit[slot, low:high, :]))
            tall_b = tall.astype(BF16)
            kern_t[at, here] = tall_b
            scaled = tall * first_stats[slot, 0:1, low:high]
            fold = scaled[:, 0:128]
            for piece in range(1, count // 128):
                fold = fold + scaled[:, piece * 128 : (piece + 1) * 128]
            vectors = wt[0, slot, :, :, low:high].reshape(vecs, count)
            product = nt(tall_b, vectors)
            if isinstance(slot, int) and slot == 0:
                means[at, :] = fold
                side[at, :] = product
            else:
                means[at, :] += fold
                side[at, :] += product
            return carry

        lax.fori_loop(0, marks // build_tile, visit, 0)

    def await_mate(slot, low=0, high=3):
        for refs, sem in chunk(slot)[low:high]:
            arrived(refs, sem.at[slot])

    build_tile = tile(marks, BUILD)
    build(0)
    await_mate(line)
    build(line)
    for t in range(line - 2):
        slot = relay(t)
        build(slot)
        await_mate(line + slot)
        build(line + slot)
    if line > 1:
        slot = relay(line - 2, 0, 2)
        build(slot, 0, half)
        relay(line - 2, 2, 3)
        await_mate(line + slot, 0, 2)
        build(line + slot, 0, half)
        build(slot, half, own)
        await_mate(line + slot, 2, 3)
        build(line + slot, half, own)

    def parts():
        return [*range(1, groups), 0]

    def send_side(step, h, j, sub):
        to(
            side_out.at[step, h, sub, j], side_in.at[step, h, sub, groups - j],
            ("side", sent_sems.at[0]), grp_sems.at[h, sub, groups - j], grp=group(j),
        )

    def first_side():
        weight_sum = jnp.zeros((1, 1), F32)
        rows = jnp.zeros((2 + HALVES, 128), F32)
        for slot in range(members):
            weight_sum = weight_sum + jnp.sum(
                first_stats[slot, 0:1, 0:own], axis=1, keepdims=True
            )
            rows = rows + first_stats[slot, :, 0:128]
        totals = [column(rows[1 + h : 2 + h, 0:128])[0:hv] for h in range(HALVES)]
        totals = jnp.concatenate(totals, axis=0)
        for j in parts():
            span = pl.ds(j * part, part)
            mean = jnp.sum(jnp.transpose(means[span, :]), axis=0, keepdims=True) / weight_sum
            mean_rows[j] = jnp.broadcast_to(mean, (8, part))
            block = jnp.transpose(side[span, :]) - totals * mean
            lead_out[j] = jnp.zeros(lead_out.shape[1:], F32)
            lead_out[j, 0:1, 0:part] = mean
            lead_out[j, 1:2, 0:128] = jnp.broadcast_to(weight_sum, (1, 128))
            lead_out[j, 2 : 2 + HALVES, 0:128] = rows[1 : 1 + HALVES, :]
            if j:
                to(
                    lead_out.at[j], lead_in.at[groups - j],
                    ("lead", sent_sems.at[1]), lead_sems.at[0, groups - j], grp=group(j),
                )
            for h in range(HALVES):
                piece = block[h * hv : (h + 1) * hv, :]
                if j == 0:
                    side_acc[h, 0] = piece
                    continue
                for sub in range(SUBS):
                    side_out[0, h, sub, j] = piece[:, sub * cut : (sub + 1) * cut].astype(BF16)
                if h == 0:
                    send_side(0, h, j, 0)
        for h in range(HALVES):
            for sub in range(h == 0, SUBS):
                for j in range(1, groups):
                    send_side(0, h, j, sub)

    def line_chunk(step, h, slot):
        return [wt.at[step, slot, h], stats.at[step - 1, h, slot]]

    def send_line(step, h, source, target, **device):
        for src, dst in zip(line_chunk(step, h, source), line_chunk(step, h, target)):
            to(src, dst, ("line", sent_sems.at[2]), wt_sems.at[h, target], **device)

    def next_side(step, h):
        for k in order:
            back = line - k
            arrived(line_chunk(step, h, back), wt_sems.at[h, back])
            send_line(step, h, back, line + back, lm=mate())

        def product(j, low, sub=None):
            vectors = [wt[step, slot, h] for slot in range(low, low + line)]
            first = j * part + (sub or 0) * cut
            return nt(
                jnp.concatenate(vectors, axis=1),
                kern_t[
                    first : first + (part if sub is None else cut),
                    low * own : (low + line) * own,
                ],
            )

        for j in parts():
            side_acc[h, j] = product(j, 0)
        for slot in range(line, members):
            arrived(line_chunk(step, h, slot), wt_sems.at[h, slot])
        rows = stats[step - 1, h, 0]
        for slot in range(1, members):
            rows = rows + stats[step - 1, h, slot]
        follow_out[step - 1, h] = rows
        for j in range(1, groups):
            to(
                follow_out.at[step - 1, h], follow_in.at[step - 1, h, groups - j],
                ("follow", sent_sems.at[3]), grp_sems.at[h, 2 * SUBS, groups - j], grp=group(j),
            )
        totals = column(rows[0:1, :])[0:hv]
        for sub in range(SUBS):
            at = slice(sub * cut, (sub + 1) * cut)
            for j in parts():
                block = side_acc[h, j, :, at] + product(j, line, sub)
                block = block - totals * mean_rows[j, 0:1, at]
                if j:
                    side_out[step, h, sub, j] = block.astype(BF16)
                    send_side(step, h, j, sub)
                else:
                    side_acc[h, 0, :, at] = block

    def flat(rows, height):
        pad = -height % 8
        return jnp.concatenate(rows + [jnp.zeros_like(rows[0])] * pad, axis=0)

    def gather_side(step, h, shared):
        if step == 0 and h == 0:
            said = [lead_out[0]]
            for j in range(1, groups):
                arrived(lead_in.at[j], lead_sems.at[0, j])
                said.append(lead_in[j])
            all_weight = sum(s[1:2, 0:1] for s in said)
            mean_row = sum(s[0:1, 0:part] * (s[1:2, 0:1] / all_weight) for s in said)
            mean_all[0] = mean_row
            for j in range(1, groups):
                to(
                    mean_all.at[0], mean_all.at[groups - j],
                    ("mean", sent_sems.at[4]), lead_sems.at[1, groups - j], grp=group(j),
                )
            shared["gaps"] = flat([s[0:1, 0:part] - mean_row for s in said], groups)
            shared["totals"] = [
                [s[2 + i : 3 + i, 0:128] for s in said] for i in range(HALVES)
            ]
        factor = None
        if step == 0:
            totals = shared["totals"][h]
        else:
            said = [follow_out[step - 1, h]]
            for j in range(1, groups):
                arrived(follow_in.at[step - 1, h, j], grp_sems.at[h, 2 * SUBS, j])
                said.append(follow_in[step - 1, h, j])
            totals = [s[0:1, :] for s in said]
            factor = column(
                1.0 / jnp.sqrt(sum(s[1:2, :] for s in said) / total_rows + 1e-06)
            )[0:hv]
        correction = lax.dot_general(
            flat(totals, groups), shared["gaps"],
            (((0,), (0,)), ((), ())), precision=HIGHEST, preferred_element_type=F32,
        )[0:hv]
        for sub in range(SUBS):
            at = slice(sub * cut, (sub + 1) * cut)
            summed = side_acc[h, 0, :, at] + correction[:, at]
            for j in range(1, groups):
                arrived(side_in.at[step, h, sub, j], grp_sems.at[h, sub, j])
                summed = summed + side_in[step, h, sub, j].astype(F32)
            if factor is not None:
                summed = summed * factor
            side_b[step, h, sub, 0] = summed.astype(BF16)
            for j in range(1, groups):
                to(
                    side_b.at[step, h, sub, 0], side_b.at[step, h, sub, groups - j],
                    ("gather", sent_sems.at[5]), grp_sems.at[h, SUBS + sub, groups - j],
                    grp=group(j),
                )

    wide = 2 if line % 2 == 0 else 1

    def make_image(step, h):
        if step == 0 and h == 0:
            for j in range(1, groups):
                arrived(mean_all.at[j], lead_sems.at[1, j])
        weighed = jnp.zeros((hv, part), F32)
        blocks = []
        for sub in range(SUBS):
            for j in range(1, groups):
                arrived(side_b.at[step, h, sub, j], grp_sems.at[h, SUBS + sub, j])
        for j in range(groups):
            blocks.append(jnp.concatenate(
                [side_b[step, h, sub, j] for sub in range(SUBS)], axis=1
            ))
            weighed = weighed + blocks[j].astype(F32) * mean_all[j, 0:1, :]
        shift = jnp.sum(weighed, axis=1, keepdims=True)
        whole = jnp.concatenate(blocks, axis=1)

        def product(slot):
            result = nn(whole, kern_t[:, slot * own : (slot + wide) * own]) - shift
            return [result[:, i * own : (i + 1) * own] for i in range(wide)]

        starts = range(line - wide, -1, -wide)
        for start in starts:
            pieces = product(line + start)
            for i in reversed(range(wide)):
                k = start + i
                image_out[step, h, k] = pieces[i].astype(BF16)
                to(
                    image_out.at[step, h, k], pair_in.at[step, h, k],
                    ("pair", sent_sems.at[6]), img_sems.at[h, 0, k], lm=mate(),
                )
        for start in starts:
            pieces = product(start)
            for i in reversed(range(wide)):
                k = start + i
                arrived(pair_in.at[step, h, k], img_sems.at[h, 0, k])
                mine = pieces[i] + pair_in[step, h, k].astype(F32)
                if k == 0:
                    held[h] = mine
                    continue
                line_out[step, h, k] = mine.astype(BF16)
                to(
                    line_out.at[step, h, k], line_in.at[step, h, line - k],
                    ("sum", sent_sems.at[7]), img_sems.at[h, 1, line - k], lm=along(k),
                )

    def end_image(step, h):
        image = held[h]
        for k in order:
            arrived(line_in.at[step, h, line - k], img_sems.at[h, 1, line - k])
            image = image + line_in[step, h, line - k].astype(F32)
        image = weight_row * image
        square = jnp.sum(image * image, axis=1, keepdims=True)
        if step == ITERS - 1:
            held[h] = image
            return square
        full = weight_row * image
        wt[step + 1, 0, h] = full.astype(BF16)
        rows = stat_rows([jnp.sum(full, axis=1, keepdims=True), square])
        stats[step, h, 0] = jnp.zeros((2, 128), F32)
        stats[step, h, 0, :, 0:hv] = rows[0:2, :]
        send_line(step + 1, h, 0, line, lm=mate())
        for k in order:
            send_line(step + 1, h, 0, line - k, lm=along(k))
        return square

    shared = {}
    squares = []
    for step in range(ITERS):
        if step == 0:
            first_side()
        else:
            for h in range(HALVES):
                next_side(step, h)
        for h in range(HALVES):
            gather_side(step, h, shared)
        for h in range(HALVES):
            make_image(step, h)
        squares = [end_image(step, h) for h in range(HALVES)]

    square = stat_rows([jnp.concatenate(squares, axis=0)])[0:1, :]
    norms[0] = square
    others = [(j, k) for j in range(groups) for k in range(members)][1:]
    for j, k in others:
        there = (groups - j) % groups * members + (members - k) % members
        to(
            norms.at[0], norms.at[there], ("norm", sent_sems.at[8]), norm_sems.at[there],
            grp=group(j), lm=(me_l + k) % members,
        )
    for j, k in others:
        arrived(norms.at[j * members + k], norm_sems.at[j * members + k])
    square = jnp.sum(norms[:, 0, :], axis=0, keepdims=True)
    image = jnp.transpose(jnp.concatenate([held[h] for h in range(HALVES)], axis=0))
    out_ref[...] = image / jnp.sqrt(square / total_rows + 1e-06)
    for when, sem, total in sends.values():
        wait = waiter(bytes_of(total), sem).wait_send
        if when is None:
            wait()
        else:
            pl.when(when)(wait)


def local(groups, members, embeddings, landmarks, start_vectors, row_weight, spread):
    own, width = embeddings.shape
    marks = landmarks.shape[0]
    vecs = start_vectors.shape[1]
    rows = own * members
    part = marks // groups
    line = members // 2
    hv = vecs // HALVES
    wide = max(own, 128)
    span = max(part, 128)
    vmem = pl.BlockSpec(memory_space=pltpu.VMEM)
    dma = pltpu.SemaphoreType.DMA
    return pl.pallas_call(
        functools.partial(kernel, groups, members),
        out_shape=jax.ShapeDtypeStruct((own, vecs), F32),
        in_specs=[pl.BlockSpec(memory_space=pl.ANY)] * 5,
        out_specs=vmem,
        scratch_shapes=[
            pltpu.SMEM((1,), F32),
            pltpu.VMEM((own, width), BF16),
            pltpu.VMEM((own, vecs), F32),
            pltpu.VMEM((1, own), F32),
            pltpu.VMEM((marks, width), BF16),
            pltpu.VMEM((marks, width), BF16),
            pltpu.VMEM((marks, rows), BF16),
            pltpu.VMEM((members, own, width), BF16),
            pltpu.VMEM((ITERS, members, HALVES, hv, own), BF16),
            pltpu.VMEM((members, 2 + HALVES, wide), F32),
            pltpu.VMEM((ITERS - 1, HALVES, members, 2, 128), F32),
            pltpu.VMEM((marks, vecs), F32),
            pltpu.VMEM((marks, 128), F32),
            pltpu.VMEM((groups, 8, part), F32),
            pltpu.VMEM((groups, 1, part), F32),
            pltpu.VMEM((ITERS, HALVES, SUBS, groups, hv, part // SUBS), BF16),
            pltpu.VMEM((ITERS, HALVES, SUBS, groups, hv, part // SUBS), BF16),
            pltpu.VMEM((HALVES, groups, hv, part), F32),
            pltpu.VMEM((groups, 2 + HALVES, span), F32),
            pltpu.VMEM((groups, 2 + HALVES, span), F32),
            pltpu.VMEM((ITERS - 1, HALVES, 2, 128), F32),
            pltpu.VMEM((ITERS - 1, HALVES, groups, 2, 128), F32),
            pltpu.VMEM((ITERS, HALVES, SUBS, groups, hv, part // SUBS), BF16),
            pltpu.VMEM((ITERS, HALVES, line, hv, own), BF16),
            pltpu.VMEM((ITERS, HALVES, line, hv, own), BF16),
            pltpu.VMEM((ITERS, HALVES, line, hv, own), BF16),
            pltpu.VMEM((ITERS, HALVES, line, hv, own), BF16),
            pltpu.VMEM((HALVES, hv, own), F32),
            pltpu.VMEM((groups * members, 1, vecs), F32),
            pltpu.VMEM((HALVES * members * (hv * own // 256 + 2), 1, 128), F32),
            dma((3, members)),
            dma((5 + line,)),
            dma((HALVES, members)),
            dma((2, groups)),
            dma((HALVES, 2 * SUBS + 1, groups)),
            dma((HALVES, 2, line)),
            dma((groups * members,)),
            dma((9,)),
            dma((groups,)),
            dma((4,)),
        ],
        compiler_params=pltpu.CompilerParams(
            collective_id=0, has_side_effects=True, vmem_limit_bytes=62 * 2**20
        ),
    )(spread, embeddings, landmarks, start_vectors, row_weight.reshape(1, own))


def solution(mesh):
    groups, members = mesh.shape["grp"], mesh.shape["lm"]
    in_specs = (
        P(("grp", "lm"), None),
        P("lm", None),
        P(("grp", "lm"), None),
        P(("grp", "lm")),
        P(),
    )
    return jax.shard_map(
        functools.partial(local, groups, members), mesh=mesh, in_specs=in_specs,
        out_specs=P(("grp", "lm"), None), check_vma=False,
    )
```

```python
import functools
import math

import jax
import jax.numpy as jnp
from jax import lax
from jax.experimental import pallas as pl
from jax.experimental.pallas import tpu as pltpu
from jax.sharding import PartitionSpec as P

ITERS = 2
HALVES = 2
SUBS = 1
F32 = jnp.float32
BF16 = jnp.bfloat16
BUILD = 1024
HIGHEST = lax.Precision.HIGHEST


def nt(a, b):
    return lax.dot_general(a, b, (((1,), (1,)), ((), ())), preferred_element_type=F32)


def nn(a, b):
    return jnp.dot(a, b, preferred_element_type=F32)


def tile(total, most):
    size = min(total, most)
    while total % size:
        size -= 8
    return size


def rows_at(index, size):
    return pl.ds(pl.multiple_of(index * size, size), size)


def column(row):
    return jnp.transpose(jnp.broadcast_to(row, (128, row.shape[1])))[:, 0:1]


def visits(z, line):
    left, right = z, line - 1 - z
    found = []
    for ahead, behind, from_left in ((left, right, True), (right, left, False)):
        for d in range(1, ahead + 1):
            if d == 1:
                key = 1 if ahead <= behind else 2
            elif d == 2:
                key = 0 if behind else line + 1
            else:
                key = d + 1
            found.append((key, d, from_left))
    return [(d, from_left) for _, d, from_left in sorted(found)]


def kernel(
    groups, members, spread_hbm, emb_hbm, marks_ref, vec_hbm, weight_hbm, out_ref,
    spread_ref, emb_ref, vec_ref, weight_ref, marks_in, marks_unit, kern_t, unit, wt, first_stats, stats, side, means, mean_rows,
    mean_all, side_out, side_in, side_acc, lead_out, lead_in, follow_out, follow_in,
    side_b, image_out, pair_in, line_out, line_in, held, norms, gauge,
    row_sems, own_sems, wt_sems, lead_sems, grp_sems, img_sems, norm_sems, sent_sems,
    mark_sems, in_sems,
):
    own, width = emb_ref.shape
    marks = marks_ref.shape[0]
    vecs = vec_ref.shape[1]
    part = marks // groups
    line = members // 2
    total_rows = own * groups * members
    hv = vecs // HALVES
    me_g = lax.axis_index("grp")
    me_l = lax.axis_index("lm")
    z = me_l // 2
    c = me_l % 2
    half = own // 2
    cut = part // SUBS
    sends = {}

    def size(ref):
        return math.prod(ref.shape) * jnp.dtype(ref.dtype).itemsize

    def to(src, dst, send_sem, recv_sem, when=None, **device):
        name, sem = send_sem
        copy = pltpu.make_async_remote_copy(
            src_ref=src, dst_ref=dst, send_sem=sem, recv_sem=recv_sem,
            device_id=device, device_id_type=pl.DeviceIdType.MESH,
        )
        if when is None:
            copy.start()
        else:
            pl.when(when)(copy.start)
        _, _, total = sends.get(name, (None, None, 0))
        sends[name] = (when, sem, total + size(src))

    def bytes_of(total):
        unit = 16 * 128 * 2
        if total % unit:
            return gauge.at[pl.ds(0, total // 512)]
        blocks = total // unit
        across = 1
        while blocks % across or blocks // across > marks // 16:
            across += 1
        return kern_t.at[pl.ds(0, blocks // across * 16), pl.ds(0, across * 128)]

    def waiter(ref, sem):
        return pltpu.make_async_remote_copy(
            src_ref=ref, dst_ref=ref, send_sem=sem, recv_sem=sem,
            device_id={"lm": me_l}, device_id_type=pl.DeviceIdType.MESH,
        )

    def arrived(refs, sem):
        refs = refs if isinstance(refs, list) else [refs]
        ref = refs[0] if len(refs) == 1 else bytes_of(sum(map(size, refs)))
        waiter(ref, sem).wait_recv()

    def mate():
        return z * 2 + 1 - c

    def along(k):
        return (z + k) % line * 2 + c

    def group(j):
        return (me_g + j) % groups

    order = sorted(range(1, line), key=lambda k: min(k, line - k))

    barrier = pltpu.get_barrier_semaphore()
    for k in range(1, members):
        pl.semaphore_signal(
            barrier, inc=1, device_id={"lm": (me_l + k) % members},
            device_id_type=pl.DeviceIdType.MESH,
        )
    for j in range(1, groups):
        pl.semaphore_signal(
            barrier, inc=1, device_id={"grp": group(j)}, device_id_type=pl.DeviceIdType.MESH
        )

    inputs = []
    for i, (src, dst) in enumerate((
        (emb_hbm, emb_ref), (weight_hbm, weight_ref), (vec_hbm, vec_ref),
        (spread_hbm, spread_ref),
    )):
        inputs.append(pltpu.make_async_copy(src, dst, in_sems.at[i]))
        inputs[i].start()
    mark_copies = []
    for j in range(groups):
        mark_copies.append(pltpu.make_async_copy(
            marks_ref.at[pl.ds(pl.multiple_of(group(j) * part, part), part), :],
            marks_in.at[pl.ds(j * part, part), :], mark_sems.at[j],
        ))
        mark_copies[j].start()

    inputs[0].wait()
    values = emb_ref[...].astype(F32)
    scale = lax.rsqrt(jnp.sum(values * values, axis=1, keepdims=True) + 1e-06)
    unit[0] = (values * scale).astype(BF16)

    def stat_rows(columns):
        lane = lax.broadcasted_iota(jnp.int32, (columns[0].shape[0], 128), 1)
        wide = jnp.zeros(lane.shape, F32)
        for i, col in enumerate(columns):
            wide = jnp.where(lane == i, col, wide)
        return jnp.transpose(wide)[0:8, :]

    for copy in inputs[1:]:
        copy.wait()
    gamma = spread_ref[0]
    weight_row = weight_ref[...]
    full = weight_row * jnp.transpose(vec_ref[...])
    first_stats[0] = jnp.zeros(first_stats.shape[1:], F32)
    first_stats[0, 0:1, 0:own] = weight_row
    for h in range(HALVES):
        piece = full[h * hv : (h + 1) * hv, :]
        wt[0, 0, h] = piece.astype(BF16)
        first_stats[0, 1 + h : 2 + h, 0:hv] = stat_rows(
            [jnp.sum(piece, axis=1, keepdims=True)]
        )[0:1, :]
    pl.semaphore_wait(barrier, members - 1 + groups - 1)

    def chunk(slot):
        return [
            ([wt.at[0, slot], first_stats.at[slot]], row_sems.at[0]),
            ([unit.at[slot, pl.ds(0, half), :]], row_sems.at[1]),
            ([unit.at[slot, pl.ds(half, half), :]], row_sems.at[2]),
        ]

    def send(sources, targets, name, sem, slot, when=None, **device):
        for (srcs, _), (dsts, recv) in zip(sources, targets):
            for src, dst in zip(srcs, dsts):
                to(src, dst, (name, sem), recv.at[slot], when, **device)

    def send_own():
        send(chunk(0), chunk(line), "mate", own_sems.at[0], line, lm=mate())
        for d, early in ((2, True), (1, False), (2, False)):
            if d < line:
                for right in (1, 0):
                    slot = line - d if right else d
                    goes = z < line - d if right else z >= d
                    relayed = z < line - 3 if right else z >= 3
                    if d == 2:
                        goes = relayed if early else goes & ~relayed
                    send(
                        chunk(0), chunk(slot), f"own {d} {right} {early}",
                        own_sems.at[2 * d + right - 1], slot, when=goes,
                        lm=(z + d if right else z + line - d) % line * 2 + c,
                    )

    send_own()

    mark_tile = tile(part, 256)

    def unit_marks(i, carry):
        at = rows_at(i, mark_tile)
        block = marks_in[at, :].astype(F32)
        factor = lax.rsqrt(jnp.sum(block * block, axis=1, keepdims=True) + 1e-06)
        marks_unit[at, :] = (block * factor).astype(BF16)
        return carry

    for j in range(groups):
        mark_copies[j].wait()
        lax.fori_loop(
            j * part // mark_tile, (j + 1) * part // mark_tile, unit_marks, 0
        )

    def at_z(table):
        found = jnp.int32(table[0])
        for position in range(1, line):
            found = jnp.where(z == position, jnp.int32(table[position]), found)
        return found

    def relay(t, low=0, high=3):
        plan = [visits(position, line)[t] for position in range(line)]
        slot = at_z([line - d if left else d for d, left in plan])
        left = at_z([int(left) for _, left in plan]) == 1
        more = at_z([
            int(d >= 2 and (position < line - 1 if left else position > 0))
            for position, (d, left) in enumerate(plan)
        ]) == 1
        follow = jnp.where(more, jnp.where(left, slot - 1, slot + 1), slot)
        for source, target in zip(chunk(slot)[low:high], chunk(follow)[low:high]):
            arrived(source[0], source[1].at[slot])
            send(
                [source], [target], f"relay {t}", own_sems.at[5 + t], follow, when=more,
                lm=jnp.where(left, z + 1, z - 1 + line) % line * 2 + c,
            )
        send(
            chunk(slot)[low:high], chunk(line + slot)[low:high], "mate", own_sems.at[0],
            line + slot, lm=mate(),
        )
        return slot

    def build(slot, low=0, high=own):
        count = high - low
        here = pl.ds(pl.multiple_of(slot * own + low, math.gcd(own, 128)), count)

        def visit(i, carry):
            at = rows_at(i, build_tile)
            tall = jnp.exp(gamma * nt(marks_unit[at, :], unit[slot, low:high, :]))
            tall_b = tall.astype(BF16)
            kern_t[at, here] = tall_b
            scaled = tall * first_stats[slot, 0:1, low:high]
            fold = scaled[:, 0:128]
            for piece in range(1, count // 128):
                fold = fold + scaled[:, piece * 128 : (piece + 1) * 128]
            vectors = wt[0, slot, :, :, low:high].reshape(vecs, count)
            product = nt(tall_b, vectors)
            if isinstance(slot, int) and slot == 0:
                means[at, :] = fold
                side[at, :] = product
            else:
                means[at, :] += fold
                side[at, :] += product
            return carry

        lax.fori_loop(0, marks // build_tile, visit, 0)

    def await_mate(slot, low=0, high=3):
        for refs, sem in chunk(slot)[low:high]:
            arrived(refs, sem.at[slot])

    build_tile = tile(marks, BUILD)
    build(0)
    await_mate(line)
    build(line)
    for t in range(line - 2):
        slot = relay(t)
        build(slot)
        await_mate(line + slot)
        build(line + slot)
    if line > 1:
        slot = relay(line - 2, 0, 2)
        build(slot, 0, half)
        await_mate(line + slot, 0, 2)
        build(line + slot, 0, half)
        relay(line - 2, 2, 3)
        build(slot, half, own)
        await_mate(line + slot, 2, 3)
        build(line + slot, half, own)

    def parts():
        return [*range(1, groups), 0]

    def send_side(step, h, j, sub):
        to(
            side_out.at[step, h, sub, j], side_in.at[step, h, sub, groups - j],
            ("side", sent_sems.at[0]), grp_sems.at[h, sub, groups - j], grp=group(j),
        )

    def first_side():
        weight_sum = jnp.zeros((1, 1), F32)
        rows = jnp.zeros((2 + HALVES, 128), F32)
        for slot in range(members):
            weight_sum = weight_sum + jnp.sum(
                first_stats[slot, 0:1, 0:own], axis=1, keepdims=True
            )
            rows = rows + first_stats[slot, :, 0:128]
        totals = [column(rows[1 + h : 2 + h, 0:128])[0:hv] for h in range(HALVES)]
        totals = jnp.concatenate(totals, axis=0)
        for j in parts():
            span = pl.ds(j * part, part)
            mean = jnp.sum(jnp.transpose(means[span, :]), axis=0, keepdims=True) / weight_sum
            mean_rows[j] = jnp.broadcast_to(mean, (8, part))
            block = jnp.transpose(side[span, :]) - totals * mean
            lead_out[j] = jnp.zeros(lead_out.shape[1:], F32)
            lead_out[j, 0:1, 0:part] = mean
            lead_out[j, 1:2, 0:128] = jnp.broadcast_to(weight_sum, (1, 128))
            lead_out[j, 2 : 2 + HALVES, 0:128] = rows[1 : 1 + HALVES, :]
            if j:
                to(
                    lead_out.at[j], lead_in.at[groups - j],
                    ("lead", sent_sems.at[1]), lead_sems.at[0, groups - j], grp=group(j),
                )
            for h in range(HALVES):
                piece = block[h * hv : (h + 1) * hv, :]
                if j == 0:
                    side_acc[h, 0] = piece
                    continue
                for sub in range(SUBS):
                    side_out[0, h, sub, j] = piece[:, sub * cut : (sub + 1) * cut].astype(BF16)
                if h == 0:
                    send_side(0, h, j, 0)
        for h in range(HALVES):
            for sub in range(h == 0, SUBS):
                for j in range(1, groups):
                    send_side(0, h, j, sub)

    def line_chunk(step, h, slot):
        return [wt.at[step, slot, h], stats.at[step - 1, h, slot]]

    def send_line(step, h, source, target, **device):
        for src, dst in zip(line_chunk(step, h, source), line_chunk(step, h, target)):
            to(src, dst, ("line", sent_sems.at[2]), wt_sems.at[h, target], **device)

    def next_side(step, h):
        for k in order:
            back = line - k
            arrived(line_chunk(step, h, back), wt_sems.at[h, back])
            send_line(step, h, back, line + back, lm=mate())

        def product(j, low, sub=None):
            vectors = [wt[step, slot, h] for slot in range(low, low + line)]
            first = j * part + (sub or 0) * cut
            return nt(
                jnp.concatenate(vectors, axis=1),
                kern_t[
                    first : first + (part if sub is None else cut),
                    low * own : (low + line) * own,
                ],
            )

        for j in parts():
            side_acc[h, j] = product(j, 0)
        for slot in range(line, members):
            arrived(line_chunk(step, h, slot), wt_sems.at[h, slot])
        rows = stats[step - 1, h, 0]
        for slot in range(1, members):
            rows = rows + stats[step - 1, h, slot]
        follow_out[step - 1, h] = rows
        for j in range(1, groups):
            to(
                follow_out.at[step - 1, h], follow_in.at[step - 1, h, groups - j],
                ("follow", sent_sems.at[3]), grp_sems.at[h, 2 * SUBS, groups - j], grp=group(j),
            )
        totals = column(rows[0:1, :])[0:hv]
        for sub in range(SUBS):
            at = slice(sub * cut, (sub + 1) * cut)
            for j in parts():
                block = side_acc[h, j, :, at] + product(j, line, sub)
                block = block - totals * mean_rows[j, 0:1, at]
                if j:
                    side_out[step, h, sub, j] = block.astype(BF16)
                    send_side(step, h, j, sub)
                else:
                    side_acc[h, 0, :, at] = block

    def flat(rows, height):
        pad = -height % 8
        return jnp.concatenate(rows + [jnp.zeros_like(rows[0])] * pad, axis=0)

    def gather_side(step, h, shared):
        if step == 0 and h == 0:
            said = [lead_out[0]]
            for j in range(1, groups):
                arrived(lead_in.at[j], lead_sems.at[0, j])
                said.append(lead_in[j])
            all_weight = sum(s[1:2, 0:1] for s in said)
            mean_row = sum(s[0:1, 0:part] * (s[1:2, 0:1] / all_weight) for s in said)
            mean_all[0] = mean_row
            for j in range(1, groups):
                to(
                    mean_all.at[0], mean_all.at[groups - j],
                    ("mean", sent_sems.at[4]), lead_sems.at[1, groups - j], grp=group(j),
                )
            shared["gaps"] = flat([s[0:1, 0:part] - mean_row for s in said], groups)
            shared["totals"] = [
                [s[2 + i : 3 + i, 0:128] for s in said] for i in range(HALVES)
            ]
        factor = None
        if step == 0:
            totals = shared["totals"][h]
        else:
            said = [follow_out[step - 1, h]]
            for j in range(1, groups):
                arrived(follow_in.at[step - 1, h, j], grp_sems.at[h, 2 * SUBS, j])
                said.append(follow_in[step - 1, h, j])
            totals = [s[0:1, :] for s in said]
            factor = column(
                1.0 / jnp.sqrt(sum(s[1:2, :] for s in said) / total_rows + 1e-06)
            )[0:hv]
        correction = lax.dot_general(
            flat(totals, groups), shared["gaps"],
            (((0,), (0,)), ((), ())), precision=HIGHEST, preferred_element_type=F32,
        )[0:hv]
        for sub in range(SUBS):
            at = slice(sub * cut, (sub + 1) * cut)
            summed = side_acc[h, 0, :, at] + correction[:, at]
            for j in range(1, groups):
                arrived(side_in.at[step, h, sub, j], grp_sems.at[h, sub, j])
                summed = summed + side_in[step, h, sub, j].astype(F32)
            if factor is not None:
                summed = summed * factor
            side_b[step, h, sub, 0] = summed.astype(BF16)
            for j in range(1, groups):
                to(
                    side_b.at[step, h, sub, 0], side_b.at[step, h, sub, groups - j],
                    ("gather", sent_sems.at[5]), grp_sems.at[h, SUBS + sub, groups - j],
                    grp=group(j),
                )

    wide = 2 if line % 2 == 0 else 1

    def make_image(step, h):
        if step == 0 and h == 0:
            for j in range(1, groups):
                arrived(mean_all.at[j], lead_sems.at[1, j])
        weighed = jnp.zeros((hv, part), F32)
        blocks = []
        for sub in range(SUBS):
            for j in range(1, groups):
                arrived(side_b.at[step, h, sub, j], grp_sems.at[h, SUBS + sub, j])
        for j in range(groups):
            blocks.append(jnp.concatenate(
                [side_b[step, h, sub, j] for sub in range(SUBS)], axis=1
            ))
            weighed = weighed + blocks[j].astype(F32) * mean_all[j, 0:1, :]
        shift = jnp.sum(weighed, axis=1, keepdims=True)
        whole = jnp.concatenate(blocks, axis=1)

        def product(slot):
            result = nn(whole, kern_t[:, slot * own : (slot + wide) * own]) - shift
            return [result[:, i * own : (i + 1) * own] for i in range(wide)]

        starts = range(line - wide, -1, -wide)
        for start in starts:
            pieces = product(line + start)
            for i in reversed(range(wide)):
                k = start + i
                image_out[step, h, k] = pieces[i].astype(BF16)
                to(
                    image_out.at[step, h, k], pair_in.at[step, h, k],
                    ("pair", sent_sems.at[6]), img_sems.at[h, 0, k], lm=mate(),
                )
        for start in starts:
            pieces = product(start)
            for i in reversed(range(wide)):
                k = start + i
                arrived(pair_in.at[step, h, k], img_sems.at[h, 0, k])
                mine = pieces[i] + pair_in[step, h, k].astype(F32)
                if k == 0:
                    held[h] = mine
                    continue
                line_out[step, h, k] = mine.astype(BF16)
                to(
                    line_out.at[step, h, k], line_in.at[step, h, line - k],
                    ("sum", sent_sems.at[7]), img_sems.at[h, 1, line - k], lm=along(k),
                )

    def end_image(step, h):
        image = held[h]
        for k in order:
            arrived(line_in.at[step, h, line - k], img_sems.at[h, 1, line - k])
            image = image + line_in[step, h, line - k].astype(F32)
        image = weight_row * image
        square = jnp.sum(image * image, axis=1, keepdims=True)
        if step == ITERS - 1:
            held[h] = image
            return square
        full = weight_row * image
        wt[step + 1, 0, h] = full.astype(BF16)
        rows = stat_rows([jnp.sum(full, axis=1, keepdims=True), square])
        stats[step, h, 0] = jnp.zeros((2, 128), F32)
        stats[step, h, 0, :, 0:hv] = rows[0:2, :]
        send_line(step + 1, h, 0, line, lm=mate())
        for k in order:
            send_line(step + 1, h, 0, line - k, lm=along(k))
        return square

    shared = {}
    squares = []
    for step in range(ITERS):
        if step == 0:
            first_side()
        else:
            for h in range(HALVES):
                next_side(step, h)
        for h in range(HALVES):
            gather_side(step, h, shared)
        for h in range(HALVES):
            make_image(step, h)
        squares = [end_image(step, h) for h in range(HALVES)]

    square = stat_rows([jnp.concatenate(squares, axis=0)])[0:1, :]
    norms[0] = square
    others = [(j, k) for j in range(groups) for k in range(members)][1:]
    for j, k in others:
        there = (groups - j) % groups * members + (members - k) % members
        to(
            norms.at[0], norms.at[there], ("norm", sent_sems.at[8]), norm_sems.at[there],
            grp=group(j), lm=(me_l + k) % members,
        )
    for j, k in others:
        arrived(norms.at[j * members + k], norm_sems.at[j * members + k])
    square = jnp.sum(norms[:, 0, :], axis=0, keepdims=True)
    image = jnp.transpose(jnp.concatenate([held[h] for h in range(HALVES)], axis=0))
    out_ref[...] = image / jnp.sqrt(square / total_rows + 1e-06)
    for when, sem, total in sends.values():
        wait = waiter(bytes_of(total), sem).wait_send
        if when is None:
            wait()
        else:
            pl.when(when)(wait)


def local(groups, members, embeddings, landmarks, start_vectors, row_weight, spread):
    own, width = embeddings.shape
    marks = landmarks.shape[0]
    vecs = start_vectors.shape[1]
    rows = own * members
    part = marks // groups
    line = members // 2
    hv = vecs // HALVES
    wide = max(own, 128)
    span = max(part, 128)
    vmem = pl.BlockSpec(memory_space=pltpu.VMEM)
    dma = pltpu.SemaphoreType.DMA
    return pl.pallas_call(
        functools.partial(kernel, groups, members),
        out_shape=pltpu.VMEM((own, vecs), F32),
        in_specs=[pl.BlockSpec(memory_space=pl.ANY)] * 5,
        out_specs=vmem,
        scratch_shapes=[
            pltpu.SMEM((1,), F32),
            pltpu.VMEM((own, width), BF16),
            pltpu.VMEM((own, vecs), F32),
            pltpu.VMEM((1, own), F32),
            pltpu.VMEM((marks, width), BF16),
            pltpu.VMEM((marks, width), BF16),
            pltpu.VMEM((marks, rows), BF16),
            pltpu.VMEM((members, own, width), BF16),
            pltpu.VMEM((ITERS, members, HALVES, hv, own), BF16),
            pltpu.VMEM((members, 2 + HALVES, wide), F32),
            pltpu.VMEM((ITERS - 1, HALVES, members, 2, 128), F32),
            pltpu.VMEM((marks, vecs), F32),
            pltpu.VMEM((marks, 128), F32),
            pltpu.VMEM((groups, 8, part), F32),
            pltpu.VMEM((groups, 1, part), F32),
            pltpu.VMEM((ITERS, HALVES, SUBS, groups, hv, part // SUBS), BF16),
            pltpu.VMEM((ITERS, HALVES, SUBS, groups, hv, part // SUBS), BF16),
            pltpu.VMEM((HALVES, groups, hv, part), F32),
            pltpu.VMEM((groups, 2 + HALVES, span), F32),
            pltpu.VMEM((groups, 2 + HALVES, span), F32),
            pltpu.VMEM((ITERS - 1, HALVES, 2, 128), F32),
            pltpu.VMEM((ITERS - 1, HALVES, groups, 2, 128), F32),
            pltpu.VMEM((ITERS, HALVES, SUBS, groups, hv, part // SUBS), BF16),
            pltpu.VMEM((ITERS, HALVES, line, hv, own), BF16),
            pltpu.VMEM((ITERS, HALVES, line, hv, own), BF16),
            pltpu.VMEM((ITERS, HALVES, line, hv, own), BF16),
            pltpu.VMEM((ITERS, HALVES, line, hv, own), BF16),
            pltpu.VMEM((HALVES, hv, own), F32),
            pltpu.VMEM((groups * members, 1, vecs), F32),
            pltpu.VMEM((HALVES * members * (hv * own // 256 + 2), 1, 128), F32),
            dma((3, members)),
            dma((5 + line,)),
            dma((HALVES, members)),
            dma((2, groups)),
            dma((HALVES, 2 * SUBS + 1, groups)),
            dma((HALVES, 2, line)),
            dma((groups * members,)),
            dma((9,)),
            dma((groups,)),
            dma((4,)),
        ],
        compiler_params=pltpu.CompilerParams(
            collective_id=0, has_side_effects=True, vmem_limit_bytes=62 * 2**20
        ),
    )(spread, embeddings, landmarks, start_vectors, row_weight.reshape(1, own))


def solution(mesh):
    groups, members = mesh.shape["grp"], mesh.shape["lm"]
    in_specs = (
        P(("grp", "lm"), None),
        P("lm", None),
        P(("grp", "lm"), None),
        P(("grp", "lm")),
        P(),
    )
    return jax.shard_map(
        functools.partial(local, groups, members), mesh=mesh, in_specs=in_specs,
        out_specs=P(("grp", "lm"), None), check_vma=False,
    )
```

```python
import functools
import math

import jax
import jax.numpy as jnp
from jax import lax
from jax.experimental import pallas as pl
from jax.experimental.pallas import tpu as pltpu
from jax.sharding import PartitionSpec as P

ITERS = 2
HALVES = 2
SUBS = 1
F32 = jnp.float32
BF16 = jnp.bfloat16
BUILD = 1024
HIGHEST = lax.Precision.HIGHEST


def nt(a, b):
    return lax.dot_general(a, b, (((1,), (1,)), ((), ())), preferred_element_type=F32)


def nn(a, b):
    return jnp.dot(a, b, preferred_element_type=F32)


def tile(total, most):
    size = min(total, most)
    while total % size:
        size -= 8
    return size


def rows_at(index, size):
    return pl.ds(pl.multiple_of(index * size, size), size)


def column(row):
    return jnp.transpose(jnp.broadcast_to(row, (128, row.shape[1])))[:, 0:1]


def visits(z, line):
    left, right = z, line - 1 - z
    found = []
    for ahead, behind, from_left in ((left, right, True), (right, left, False)):
        for d in range(1, ahead + 1):
            if d == 1:
                key = 1 if ahead <= behind else 2
            elif d == 2:
                key = 0 if behind else line + 1
            else:
                key = d + 1
            found.append((key, d, from_left))
    return [(d, from_left) for _, d, from_left in sorted(found)]


def kernel(
    groups, members, spread_hbm, emb_hbm, marks_ref, vec_hbm, weight_hbm, out_ref,
    spread_ref, emb_ref, vec_ref, weight_ref, marks_in, marks_unit, kern_t, unit, wt, first_stats, stats, side, means, mean_rows,
    mean_all, side_out, side_in, side_acc, lead_out, lead_in, follow_out, follow_in,
    side_b, image_out, pair_in, line_out, line_in, held, norms, gauge,
    row_sems, own_sems, wt_sems, lead_sems, grp_sems, img_sems, norm_sems, sent_sems,
    mark_sems, in_sems,
):
    own, width = emb_ref.shape
    marks = marks_ref.shape[0]
    vecs = vec_ref.shape[1]
    part = marks // groups
    line = members // 2
    total_rows = own * groups * members
    hv = vecs // HALVES
    me_g = lax.axis_index("grp")
    me_l = lax.axis_index("lm")
    z = me_l // 2
    c = me_l % 2
    half = own // 2
    cut = part // SUBS
    sends = {}

    def size(ref):
        return math.prod(ref.shape) * jnp.dtype(ref.dtype).itemsize

    def to(src, dst, send_sem, recv_sem, when=None, **device):
        name, sem = send_sem
        copy = pltpu.make_async_remote_copy(
            src_ref=src, dst_ref=dst, send_sem=sem, recv_sem=recv_sem,
            device_id=device, device_id_type=pl.DeviceIdType.MESH,
        )
        if when is None:
            copy.start()
        else:
            pl.when(when)(copy.start)
        _, _, total = sends.get(name, (None, None, 0))
        sends[name] = (when, sem, total + size(src))

    def bytes_of(total):
        unit = 16 * 128 * 2
        if total % unit:
            return gauge.at[pl.ds(0, total // 512)]
        blocks = total // unit
        across = 1
        while blocks % across or blocks // across > marks // 16:
            across += 1
        return kern_t.at[pl.ds(0, blocks // across * 16), pl.ds(0, across * 128)]

    def waiter(ref, sem):
        return pltpu.make_async_remote_copy(
            src_ref=ref, dst_ref=ref, send_sem=sem, recv_sem=sem,
            device_id={"lm": me_l}, device_id_type=pl.DeviceIdType.MESH,
        )

    def arrived(refs, sem):
        refs = refs if isinstance(refs, list) else [refs]
        ref = refs[0] if len(refs) == 1 else bytes_of(sum(map(size, refs)))
        waiter(ref, sem).wait_recv()

    def mate():
        return z * 2 + 1 - c

    def along(k):
        return (z + k) % line * 2 + c

    def group(j):
        return (me_g + j) % groups

    order = sorted(range(1, line), key=lambda k: min(k, line - k))

    barrier = pltpu.get_barrier_semaphore()
    for k in range(1, members):
        pl.semaphore_signal(
            barrier, inc=1, device_id={"lm": (me_l + k) % members},
            device_id_type=pl.DeviceIdType.MESH,
        )
    for j in range(1, groups):
        pl.semaphore_signal(
            barrier, inc=1, device_id={"grp": group(j)}, device_id_type=pl.DeviceIdType.MESH
        )

    inputs = []
    for i, (src, dst) in enumerate((
        (emb_hbm, emb_ref), (weight_hbm, weight_ref), (vec_hbm, vec_ref),
        (spread_hbm, spread_ref),
    )):
        inputs.append(pltpu.make_async_copy(src, dst, in_sems.at[i]))
        inputs[i].start()
    mark_copies = []
    for j in range(groups):
        mark_copies.append(pltpu.make_async_copy(
            marks_ref.at[pl.ds(pl.multiple_of(group(j) * part, part), part), :],
            marks_in.at[pl.ds(j * part, part), :], mark_sems.at[j],
        ))
        mark_copies[j].start()

    inputs[0].wait()
    values = emb_ref[...].astype(F32)
    scale = lax.rsqrt(jnp.sum(values * values, axis=1, keepdims=True) + 1e-06)
    unit[0] = (values * scale).astype(BF16)

    def stat_rows(columns):
        lane = lax.broadcasted_iota(jnp.int32, (columns[0].shape[0], 128), 1)
        wide = jnp.zeros(lane.shape, F32)
        for i, col in enumerate(columns):
            wide = jnp.where(lane == i, col, wide)
        return jnp.transpose(wide)[0:8, :]

    for copy in inputs[1:]:
        copy.wait()
    gamma = spread_ref[0]
    weight_row = weight_ref[...]
    full = weight_row * jnp.transpose(vec_ref[...])
    first_stats[0] = jnp.zeros(first_stats.shape[1:], F32)
    first_stats[0, 0:1, 0:own] = weight_row
    for h in range(HALVES):
        piece = full[h * hv : (h + 1) * hv, :]
        wt[0, 0, h] = piece.astype(BF16)
        first_stats[0, 1 + h : 2 + h, 0:hv] = stat_rows(
            [jnp.sum(piece, axis=1, keepdims=True)]
        )[0:1, :]
    pl.semaphore_wait(barrier, members - 1 + groups - 1)

    def chunk(slot):
        return [
            ([wt.at[0, slot], first_stats.at[slot]], row_sems.at[0]),
            ([unit.at[slot, pl.ds(0, half), :]], row_sems.at[1]),
            ([unit.at[slot, pl.ds(half, half), :]], row_sems.at[2]),
        ]

    def send(sources, targets, name, sem, slot, when=None, **device):
        for (srcs, _), (dsts, recv) in zip(sources, targets):
            for src, dst in zip(srcs, dsts):
                to(src, dst, (name, sem), recv.at[slot], when, **device)

    def send_own():
        send(chunk(0), chunk(line), "mate", own_sems.at[0], line, lm=mate())
        for d, early in ((2, True), (1, False), (2, False)):
            if d < line:
                for right in (1, 0):
                    slot = line - d if right else d
                    goes = z < line - d if right else z >= d
                    relayed = z < line - 3 if right else z >= 3
                    if d == 2:
                        goes = relayed if early else goes & ~relayed
                    send(
                        chunk(0), chunk(slot), f"own {d} {right} {early}",
                        own_sems.at[2 * d + right - 1], slot, when=goes,
                        lm=(z + d if right else z + line - d) % line * 2 + c,
                    )

    send_own()

    mark_tile = tile(part, 256)

    def unit_marks(i, carry):
        at = rows_at(i, mark_tile)
        block = marks_in[at, :].astype(F32)
        factor = lax.rsqrt(jnp.sum(block * block, axis=1, keepdims=True) + 1e-06)
        marks_unit[at, :] = (block * factor).astype(BF16)
        return carry

    for j in range(groups):
        mark_copies[j].wait()
        lax.fori_loop(
            j * part // mark_tile, (j + 1) * part // mark_tile, unit_marks, 0
        )

    def at_z(table):
        found = jnp.int32(table[0])
        for position in range(1, line):
            found = jnp.where(z == position, jnp.int32(table[position]), found)
        return found

    def relay(t, low=0, high=3):
        plan = [visits(position, line)[t] for position in range(line)]
        slot = at_z([line - d if left else d for d, left in plan])
        left = at_z([int(left) for _, left in plan]) == 1
        more = at_z([
            int(d >= 2 and (position < line - 1 if left else position > 0))
            for position, (d, left) in enumerate(plan)
        ]) == 1
        follow = jnp.where(more, jnp.where(left, slot - 1, slot + 1), slot)
        for source, target in zip(chunk(slot)[low:high], chunk(follow)[low:high]):
            arrived(source[0], source[1].at[slot])
            send(
                [source], [target], f"relay {t}", own_sems.at[5 + t], follow, when=more,
                lm=jnp.where(left, z + 1, z - 1 + line) % line * 2 + c,
            )
        send(
            chunk(slot)[low:high], chunk(line + slot)[low:high], "mate", own_sems.at[0],
            line + slot, lm=mate(),
        )
        return slot

    def build(slot, low=0, high=own):
        count = high - low
        here = pl.ds(pl.multiple_of(slot * own + low, math.gcd(own, 128)), count)

        def visit(i, carry):
            at = rows_at(i, build_tile)
            tall = jnp.exp(gamma * nt(marks_unit[at, :], unit[slot, low:high, :]))
            tall_b = tall.astype(BF16)
            kern_t[at, here] = tall_b
            scaled = tall * first_stats[slot, 0:1, low:high]
            fold = scaled[:, 0:128]
            for piece in range(1, count // 128):
                fold = fold + scaled[:, piece * 128 : (piece + 1) * 128]
            vectors = wt[0, slot, :, :, low:high].reshape(vecs, count)
            product = nt(tall_b, vectors)
            if isinstance(slot, int) and slot == 0:
                means[at, :] = fold
                side[at, :] = product
            else:
                means[at, :] += fold
                side[at, :] += product
            return carry

        lax.fori_loop(0, marks // build_tile, visit, 0)

    def first_totals():
        weight_sum = jnp.zeros((1, 1), F32)
        rows = jnp.zeros((2 + HALVES, 128), F32)
        for slot in range(members):
            weight_sum = weight_sum + jnp.sum(
                first_stats[slot, 0:1, 0:own], axis=1, keepdims=True
            )
            rows = rows + first_stats[slot, :, 0:128]
        totals = [column(rows[1 + h : 2 + h, 0:128])[0:hv] for h in range(HALVES)]
        totals = jnp.concatenate(totals, axis=0)
        return weight_sum, rows, totals

    def await_mate(slot, low=0, high=3):
        for refs, sem in chunk(slot)[low:high]:
            arrived(refs, sem.at[slot])

    build_tile = tile(marks, BUILD)
    build(0)
    await_mate(line)
    build(line)
    for t in range(line - 2):
        slot = relay(t)
        build(slot)
        await_mate(line + slot)
        build(line + slot)
    if line > 1:
        slot = relay(line - 2, 0, 2)
        build(slot, 0, half)
        await_mate(line + slot, 0, 2)
        weight_sum, rows, totals = first_totals()
        build(line + slot, 0, half)
        relay(line - 2, 2, 3)
        build(slot, half, own)
        await_mate(line + slot, 2, 3)
        build(line + slot, half, own)
    else:
        weight_sum, rows, totals = first_totals()

    def parts():
        return [*range(1, groups), 0]

    def send_side(step, h, j, sub):
        to(
            side_out.at[step, h, sub, j], side_in.at[step, h, sub, groups - j],
            ("side", sent_sems.at[0]), grp_sems.at[h, sub], grp=group(j),
        )

    def first_side():
        for j in parts():
            span = pl.ds(j * part, part)
            mean = jnp.sum(jnp.transpose(means[span, :]), axis=0, keepdims=True) / weight_sum
            mean_rows[j] = jnp.broadcast_to(mean, (8, part))
            block = jnp.transpose(side[span, :]) - totals * mean
            lead_out[j] = jnp.zeros(lead_out.shape[1:], F32)
            lead_out[j, 0:1, 0:part] = mean
            lead_out[j, 1:2, 0:128] = jnp.broadcast_to(weight_sum, (1, 128))
            lead_out[j, 2 : 2 + HALVES, 0:128] = rows[1 : 1 + HALVES, :]
            if j:
                to(
                    lead_out.at[j], lead_in.at[groups - j],
                    ("lead", sent_sems.at[1]), lead_sems.at[0], grp=group(j),
                )
            for h in range(HALVES):
                piece = block[h * hv : (h + 1) * hv, :]
                if j == 0:
                    side_acc[h, 0] = piece
                    continue
                for sub in range(SUBS):
                    side_out[0, h, sub, j] = piece[:, sub * cut : (sub + 1) * cut].astype(BF16)
                if h == 0:
                    send_side(0, h, j, 0)
        for h in range(HALVES):
            for sub in range(h == 0, SUBS):
                for j in range(1, groups):
                    send_side(0, h, j, sub)

    def line_chunk(step, h, slot):
        return [wt.at[step, slot, h], stats.at[step - 1, h, slot]]

    def send_line(step, h, source, target, **device):
        for src, dst in zip(line_chunk(step, h, source), line_chunk(step, h, target)):
            to(src, dst, ("line", sent_sems.at[2]), wt_sems.at[h, min(target, line)], **device)

    def next_side(step, h):
        for k in order:
            back = line - k
            arrived(line_chunk(step, h, back), wt_sems.at[h, back])
            send_line(step, h, back, line + back, lm=mate())

        def product(j, low, sub=None):
            vectors = [wt[step, slot, h] for slot in range(low, low + line)]
            first = j * part + (sub or 0) * cut
            return nt(
                jnp.concatenate(vectors, axis=1),
                kern_t[
                    first : first + (part if sub is None else cut),
                    low * own : (low + line) * own,
                ],
            )

        for j in parts():
            side_acc[h, j] = product(j, 0)
        mates = [line_chunk(step, h, slot) for slot in range(line, members)]
        arrived([ref for pair in mates for ref in pair], wt_sems.at[h, line])
        rows = stats[step - 1, h, 0]
        for slot in range(1, members):
            rows = rows + stats[step - 1, h, slot]
        follow_out[step - 1, h] = rows
        for j in range(1, groups):
            to(
                follow_out.at[step - 1, h], follow_in.at[step - 1, h, groups - j],
                ("follow", sent_sems.at[3]), grp_sems.at[h, 2 * SUBS], grp=group(j),
            )
        totals = column(rows[0:1, :])[0:hv]
        for sub in range(SUBS):
            at = slice(sub * cut, (sub + 1) * cut)
            for j in parts():
                block = side_acc[h, j, :, at] + product(j, line, sub)
                block = block - totals * mean_rows[j, 0:1, at]
                if j:
                    side_out[step, h, sub, j] = block.astype(BF16)
                    send_side(step, h, j, sub)
                else:
                    side_acc[h, 0, :, at] = block

    def flat(rows, height):
        pad = -height % 8
        return jnp.concatenate(rows + [jnp.zeros_like(rows[0])] * pad, axis=0)

    def gather_side(step, h, shared):
        if step == 0 and h == 0:
            said = [lead_out[0]]
            arrived([lead_in.at[j] for j in range(1, groups)], lead_sems.at[0])
            for j in range(1, groups):
                said.append(lead_in[j])
            all_weight = sum(s[1:2, 0:1] for s in said)
            mean_row = sum(s[0:1, 0:part] * (s[1:2, 0:1] / all_weight) for s in said)
            mean_all[0] = mean_row
            for j in range(1, groups):
                to(
                    mean_all.at[0], mean_all.at[groups - j],
                    ("mean", sent_sems.at[4]), lead_sems.at[1], grp=group(j),
                )
            shared["gaps"] = flat([s[0:1, 0:part] - mean_row for s in said], groups)
            shared["totals"] = [
                [s[2 + i : 3 + i, 0:128] for s in said] for i in range(HALVES)
            ]
        factor = None
        if step == 0:
            totals = shared["totals"][h]
        else:
            said = [follow_out[step - 1, h]]
            arrived(
                [follow_in.at[step - 1, h, j] for j in range(1, groups)],
                grp_sems.at[h, 2 * SUBS],
            )
            for j in range(1, groups):
                said.append(follow_in[step - 1, h, j])
            totals = [s[0:1, :] for s in said]
            factor = column(
                1.0 / jnp.sqrt(sum(s[1:2, :] for s in said) / total_rows + 1e-06)
            )[0:hv]
        correction = lax.dot_general(
            flat(totals, groups), shared["gaps"],
            (((0,), (0,)), ((), ())), precision=HIGHEST, preferred_element_type=F32,
        )[0:hv]
        for sub in range(SUBS):
            at = slice(sub * cut, (sub + 1) * cut)
            summed = side_acc[h, 0, :, at] + correction[:, at]
            arrived(
                [side_in.at[step, h, sub, j] for j in range(1, groups)], grp_sems.at[h, sub]
            )
            for j in range(1, groups):
                summed = summed + side_in[step, h, sub, j].astype(F32)
            if factor is not None:
                summed = summed * factor
            side_b[step, h, sub, 0] = summed.astype(BF16)
            for j in range(1, groups):
                to(
                    side_b.at[step, h, sub, 0], side_b.at[step, h, sub, groups - j],
                    ("gather", sent_sems.at[5]), grp_sems.at[h, SUBS + sub],
                    grp=group(j),
                )

    wide = 2 if line % 2 == 0 else 1

    def make_image(step, h):
        if step == 0 and h == 0:
            arrived([mean_all.at[j] for j in range(1, groups)], lead_sems.at[1])
        weighed = jnp.zeros((hv, part), F32)
        blocks = []
        for sub in range(SUBS):
            arrived(
                [side_b.at[step, h, sub, j] for j in range(1, groups)],
                grp_sems.at[h, SUBS + sub],
            )
        for j in range(groups):
            blocks.append(jnp.concatenate(
                [side_b[step, h, sub, j] for sub in range(SUBS)], axis=1
            ))
            weighed = weighed + blocks[j].astype(F32) * mean_all[j, 0:1, :]
        shift = jnp.sum(weighed, axis=1, keepdims=True)
        whole = jnp.concatenate(blocks, axis=1)

        def product(slot):
            result = nn(whole, kern_t[:, slot * own : (slot + wide) * own]) - shift
            return [result[:, i * own : (i + 1) * own] for i in range(wide)]

        starts = range(line - wide, -1, -wide)
        for start in starts:
            pieces = product(line + start)
            for i in reversed(range(wide)):
                k = start + i
                image_out[step, h, k] = pieces[i].astype(BF16)
                to(
                    image_out.at[step, h, k], pair_in.at[step, h, k],
                    ("pair", sent_sems.at[6]), img_sems.at[h, k], lm=mate(),
                )
        for start in starts:
            pieces = product(start)
            for i in reversed(range(wide)):
                k = start + i
                arrived(pair_in.at[step, h, k], img_sems.at[h, k])
                mine = pieces[i] + pair_in[step, h, k].astype(F32)
                if k == 0:
                    held[h] = mine
                    continue
                line_out[step, h, k] = mine.astype(BF16)
                to(
                    line_out.at[step, h, k], line_in.at[step, h, line - k],
                    ("sum", sent_sems.at[7]), img_sems.at[h, line], lm=along(k),
                )

    def end_image(step, h):
        image = held[h]
        arrived([line_in.at[step, h, k] for k in order], img_sems.at[h, line])
        for k in order:
            image = image + line_in[step, h, line - k].astype(F32)
        image = weight_row * image
        square = jnp.sum(image * image, axis=1, keepdims=True)
        if step == ITERS - 1:
            held[h] = image
            return square
        full = weight_row * image
        wt[step + 1, 0, h] = full.astype(BF16)
        rows = stat_rows([jnp.sum(full, axis=1, keepdims=True), square])
        stats[step, h, 0] = jnp.zeros((2, 128), F32)
        stats[step, h, 0, :, 0:hv] = rows[0:2, :]
        send_line(step + 1, h, 0, line, lm=mate())
        for k in order:
            send_line(step + 1, h, 0, line - k, lm=along(k))
        return square

    shared = {}
    squares = []
    for step in range(ITERS):
        if step == 0:
            first_side()
        else:
            for h in range(HALVES):
                next_side(step, h)
        for h in range(HALVES):
            gather_side(step, h, shared)
        for h in range(HALVES):
            make_image(step, h)
        squares = [end_image(step, h) for h in range(HALVES)]

    square = stat_rows([jnp.concatenate(squares, axis=0)])[0:1, :]
    norms[0] = square
    others = [(j, k) for j in range(groups) for k in range(members)][1:]
    for j, k in others:
        there = (groups - j) % groups * members + (members - k) % members
        to(
            norms.at[0], norms.at[there], ("norm", sent_sems.at[8]), norm_sems.at[0],
            grp=group(j), lm=(me_l + k) % members,
        )
    arrived([norms.at[j * members + k] for j, k in others], norm_sems.at[0])
    square = jnp.sum(norms[:, 0, :], axis=0, keepdims=True)
    image = jnp.transpose(jnp.concatenate([held[h] for h in range(HALVES)], axis=0))
    out_ref[...] = image / jnp.sqrt(square / total_rows + 1e-06)
    for when, sem, total in sends.values():
        wait = waiter(bytes_of(total), sem).wait_send
        if when is None:
            wait()
        else:
            pl.when(when)(wait)


def local(groups, members, embeddings, landmarks, start_vectors, row_weight, spread):
    own, width = embeddings.shape
    marks = landmarks.shape[0]
    vecs = start_vectors.shape[1]
    rows = own * members
    part = marks // groups
    line = members // 2
    hv = vecs // HALVES
    wide = max(own, 128)
    span = max(part, 128)
    vmem = pl.BlockSpec(memory_space=pltpu.VMEM)
    dma = pltpu.SemaphoreType.DMA
    return pl.pallas_call(
        functools.partial(kernel, groups, members),
        out_shape=pltpu.VMEM((own, vecs), F32),
        in_specs=[pl.BlockSpec(memory_space=pl.ANY)] * 5,
        out_specs=vmem,
        scratch_shapes=[
            pltpu.SMEM((1,), F32),
            pltpu.VMEM((own, width), BF16),
            pltpu.VMEM((own, vecs), F32),
            pltpu.VMEM((1, own), F32),
            pltpu.VMEM((marks, width), BF16),
            pltpu.VMEM((marks, width), BF16),
            pltpu.VMEM((marks, rows), BF16),
            pltpu.VMEM((members, own, width), BF16),
            pltpu.VMEM((ITERS, members, HALVES, hv, own), BF16),
            pltpu.VMEM((members, 2 + HALVES, wide), F32),
            pltpu.VMEM((ITERS - 1, HALVES, members, 2, 128), F32),
            pltpu.VMEM((marks, vecs), F32),
            pltpu.VMEM((marks, 128), F32),
            pltpu.VMEM((groups, 8, part), F32),
            pltpu.VMEM((groups, 1, part), F32),
            pltpu.VMEM((ITERS, HALVES, SUBS, groups, hv, part // SUBS), BF16),
            pltpu.VMEM((ITERS, HALVES, SUBS, groups, hv, part // SUBS), BF16),
            pltpu.VMEM((HALVES, groups, hv, part), F32),
            pltpu.VMEM((groups, 2 + HALVES, span), F32),
            pltpu.VMEM((groups, 2 + HALVES, span), F32),
            pltpu.VMEM((ITERS - 1, HALVES, 2, 128), F32),
            pltpu.VMEM((ITERS - 1, HALVES, groups, 2, 128), F32),
            pltpu.VMEM((ITERS, HALVES, SUBS, groups, hv, part // SUBS), BF16),
            pltpu.VMEM((ITERS, HALVES, line, hv, own), BF16),
            pltpu.VMEM((ITERS, HALVES, line, hv, own), BF16),
            pltpu.VMEM((ITERS, HALVES, line, hv, own), BF16),
            pltpu.VMEM((ITERS, HALVES, line, hv, own), BF16),
            pltpu.VMEM((HALVES, hv, own), F32),
            pltpu.VMEM((groups * members, 1, vecs), F32),
            pltpu.VMEM((HALVES * members * (hv * own // 256 + 2), 1, 128), F32),
            dma((3, members)),
            dma((5 + line,)),
            dma((HALVES, line + 1)),
            dma((2,)),
            dma((HALVES, 2 * SUBS + 1)),
            dma((HALVES, line + 1)),
            dma((1,)),
            dma((9,)),
            dma((groups,)),
            dma((4,)),
        ],
        compiler_params=pltpu.CompilerParams(
            collective_id=0, has_side_effects=True, vmem_limit_bytes=62 * 2**20
        ),
    )(spread, embeddings, landmarks, start_vectors, row_weight.reshape(1, own))


def solution(mesh):
    groups, members = mesh.shape["grp"], mesh.shape["lm"]
    in_specs = (
        P(("grp", "lm"), None),
        P("lm", None),
        P(("grp", "lm"), None),
        P(("grp", "lm")),
        P(),
    )
    return jax.shard_map(
        functools.partial(local, groups, members), mesh=mesh, in_specs=in_specs,
        out_specs=P(("grp", "lm"), None), check_vma=False,
    )
```
